32 devices in a mesh: comp: 8 (over y, x, core), strip: 4 (over z).
Axes of the slice: x: 2, y: 2, z: 4, core: 2. Of those that a mesh axis runs over, the one named last changes fastest.
Arguments:
- energy: bfloat16 [1152, 64, 512], P('comp', 'strip'), may hold values from 0.049804688 to 2
- heading: float32 [1152], P('comp'), may hold values from -3.140625 to 3.140625
- growth: float32 [1152], P('comp'), may hold values from 0.005 to 0.05
- courant: float32 [1152, 2], P('comp'), may hold values from -0.45 to 0.45
- dissip: float32 [1152], replicated, may hold values from 0.05 to 0.5
- mixing: bfloat16 [1152, 1152], replicated, may hold values from -0.1875 to 0.1875
- transfer: bfloat16 [1152, 1152], replicated, may hold values from -0.046875 to 0.046875
- pattern: int32 [1152], replicated, may hold values from 0 to 1151, each once
- regime_winds: float32 [8, 2], replicated, may hold values from -8 to 8
- regime: int32 [32, 32], P('strip'), may hold values from 0 to 7
- seeds: int32 [32, 32], P('strip'), may hold values from 0 to 1023
- sea_mask: int32 [64, 512], P('strip'), may hold values 0 or 1
Outputs:
- energy_out: float32 [1152, 64, 512], P('comp', 'strip')
The draws below stay inside these ranges and needn't reach their ends.
Inputs may be any that keep to these rules, and one draw needn't show every extreme that they name: `pattern`: each component is named exactly once.
All inputs are finite; a program needn't handle non-finite values. No bound on the sum of `sea_mask` on one device may be relied on, other than what follows from the above.
Results may differ from the reference program's by a relative error of at most 0.0008.
Values may be sent and summed in bfloat16 or wider, within the bound.
No kernel may reach another device: no remote copies, remote signals or barrier semaphores. Data moves between devices by JAX's collectives and lax.ppermute only.
A program may use at most 192 MiB of HBM per device.

```python
import math
import jax
import jax.numpy as jnp
from jax import lax

ROWS_C = 2
NX = 512
SUBSTEPS = 4
TILE_ROWS = 2
TILE_COLS = 16
REGIMES = 8
K = 1152
NY = 64
TY = 32
TX = 32


def plant(entries, key, least, high):
    shape = entries.shape
    spot = [jax.random.randint(jax.random.fold_in(key, axis), (), 0, shape[axis]) for axis in range(len(shape))]
    entries = entries.at[tuple(spot)].set(least)
    longest = shape.index(max(shape))
    spot[longest] = (spot[longest] + 1) % shape[longest]
    return entries.at[tuple(spot)].set(high)


def shard_levels(stream_key, shape, split, least, largest):
    level = 1.0
    for dim, parts in split:
        steps = jax.random.uniform(jax.random.fold_in(jax.random.fold_in(stream_key, 6), dim), (parts,), jnp.float32, least / len(split), largest / len(split))
        level = level * jnp.repeat(jnp.exp(steps), shape[dim] // parts).reshape((-1,) + (1,) * (len(shape) - 1 - dim))
    return level


def bell_draw(stream_key, shape, spread, limit, kind=jnp.bfloat16):
    array = spread * jax.random.normal(stream_key, shape, jnp.float32)
    return jnp.clip(array, min=-limit, max=limit).astype(kind)


def setup_inputs(seed: int = 0) -> dict:
    splits = jax.random.split(jax.random.key(seed), 13)
    return {
        "energy": jnp.clip(jnp.exp(math.log(2.0) - 3.6927934 * jax.random.uniform(splits[0], (K, NY, NX), jnp.float32) ** shard_levels(splits[0], (K, NY, NX), ((0, 8), (1, 4)), -0.2, 0.2)), 0.049804688, 2.0).astype(jnp.bfloat16),
        "heading": jnp.clip(jax.random.uniform(splits[1], (K,), jnp.float32, -3.140625, 3.140625), -3.140625, 3.140625),
        "growth": jnp.clip(jnp.exp(math.log(0.05) - 2.3025851 * jax.random.uniform(splits[2], (K,), jnp.float32) ** shard_levels(splits[2], (K,), ((0, 8),), -0.2, 0.2)), 0.005, 0.05),
        "courant": jnp.clip(jax.random.uniform(splits[3], (K, 2), jnp.float32, -0.45, 0.45) * shard_levels(splits[3], (K, 2), ((0, 8),), -0.4, 0.0), -0.45, 0.45),
        "dissip": jnp.clip(jnp.exp(jax.random.uniform(splits[4], (K,), jnp.float32, math.log(0.05), math.log(0.5))), 0.05, 0.5),
        "mixing": bell_draw(splits[5], (K, K), K ** -0.5, 0.1875),
        "transfer": bell_draw(splits[6], (K, K), (16 * K) ** -0.5, 0.046875),
        "pattern": jax.random.permutation(splits[7], K).astype(jnp.int32),
        "regime_winds": jnp.clip(jax.random.uniform(splits[8], (REGIMES, 2), jnp.float32, -8.0, 8.0), -8.0, 8.0),
        "regime": plant(jax.random.randint(splits[9], (TY, TX), 0, REGIMES), jax.random.fold_in(splits[9], 1), 0, REGIMES - 1).astype(jnp.int32),
        "seeds": plant(jax.random.randint(splits[10], (TY, TX), 0, 1024), jax.random.fold_in(splits[10], 1), 0, 1023).astype(jnp.int32),
        "sea_mask": plant((jax.random.randint(splits[11], (NY, NX), 0, 4) < 3).astype(jnp.int32), jax.random.fold_in(splits[11], 1), 0, 1),
    }


def wind_fields(regime_winds, regime, seeds):
    base_u = jnp.take(regime_winds[:, 0], regime)
    base_v = jnp.take(regime_winds[:, 1], regime)
    tile_u = base_u + 0.25 * ((seeds % 13) - 6).astype(jnp.float32)
    tile_v = base_v + 0.4 * ((seeds % 7) - 3).astype(jnp.float32)
    wind_u = jnp.repeat(jnp.repeat(tile_u, TILE_ROWS, axis=0), TILE_COLS, axis=1)
    wind_v = jnp.repeat(jnp.repeat(tile_v, TILE_ROWS, axis=0), TILE_COLS, axis=1)
    return wind_u, wind_v


def cell_terms(spectra, mixing, transfer, pattern, dissip):
    spectrum_shape = spectra.shape
    flattened = spectra.reshape(spectrum_shape[0], -1)
    mixed_terms = jnp.dot(mixing, flattened, preferred_element_type=jnp.float32)
    partner = jnp.take(flattened, pattern, axis=0)
    product = (mixed_terms * partner.astype(jnp.float32)).astype(jnp.bfloat16)
    nonlinear = jnp.dot(transfer, product, preferred_element_type=jnp.float32)
    widened = flattened.astype(jnp.float32)
    mean_energy = jnp.sum(widened, axis=0) / spectrum_shape[0]
    result = nonlinear - dissip[:, None] * mean_energy[None, :] * widened
    return result.astype(jnp.bfloat16).reshape(spectrum_shape)


def advect(padded, sea_field, courant_x, courant_y):
    flux_y = jnp.maximum(courant_y, 0.0) * padded[..., :-1, :] + jnp.minimum(courant_y, 0.0) * padded[..., 1:, :]
    center = padded[..., 1:-1, :]
    widths = [(0, 0)] * (center.ndim - 1) + [(1, 1)]
    padded_x = jnp.pad(center, widths)
    flux_x = jnp.maximum(courant_x, 0.0) * padded_x[..., :-1] + jnp.minimum(courant_x, 0.0) * padded_x[..., 1:]
    return (center - (flux_x[..., 1:] - flux_x[..., :-1]) - (flux_y[..., 1:, :] - flux_y[..., :-1, :])) * sea_field


def reference(energy, heading, growth, courant, dissip, mixing, transfer, pattern, regime_winds, regime, seeds, sea_mask):
    wind_u, wind_v = wind_fields(regime_winds, regime, seeds)
    cosines = jnp.cos(heading)
    sines = jnp.sin(heading)
    block_count = NY // ROWS_C

    def source_block(block):
        row_start = (block * ROWS_C).astype(jnp.int32)
        spectra = lax.dynamic_slice_in_dim(energy, row_start, ROWS_C, 1)
        block_u = lax.dynamic_slice_in_dim(wind_u, row_start, ROWS_C, 0)
        block_v = lax.dynamic_slice_in_dim(wind_v, row_start, ROWS_C, 0)
        widened = spectra.astype(jnp.float32)
        drive = block_u[None] * cosines[:, None, None] + block_v[None] * sines[:, None, None]
        input_term = growth[:, None, None] * jnp.maximum(0.0, drive) * widened
        terms = cell_terms(spectra, mixing, transfer, pattern, dissip)
        return widened + input_term + terms.astype(jnp.float32)

    forced = lax.map(source_block, jnp.arange(block_count, dtype=jnp.int32))
    forced = jnp.transpose(forced, (1, 0, 2, 3)).reshape(K, NY, NX)
    sea_field = sea_mask.astype(jnp.float32)

    def propagate(packed):
        energy_field, numbers = packed
        for substep in range(SUBSTEPS):
            energy_field = advect(jnp.pad(energy_field, ((1, 1), (0, 0))), sea_field, numbers[0], numbers[1])
        return energy_field

    return lax.map(propagate, (forced, courant))
```

```python
import functools
import jax
import jax.numpy as jnp
from jax import lax
from jax.experimental import pallas as pl
from jax.experimental.pallas import tpu as pltpu
from jax.sharding import PartitionSpec as P

SUBSTEPS = 4
TILE_ROWS = 2
TILE_COLS = 16
GROUP = 16
LANES = 128
MIB = 1 << 20


def with_halo(block, sides, width):
    for axis, dim in sides:
        count = lax.axis_size(axis)
        forward = [(i, i + 1) for i in range(count - 1)]
        backward = [(target, source) for source, target in forward]
        low = lax.ppermute(
            lax.slice_in_dim(block, block.shape[dim] - width, None, axis=dim), axis, forward
        )
        high = lax.ppermute(lax.slice_in_dim(block, 0, width, axis=dim), axis, backward)
        block = jnp.concatenate([low, block, high], axis=dim)
    return block


def strip_winds(regime_winds, regime, seeds):
    levels = jnp.arange(regime_winds.shape[0], dtype=jnp.int32)
    onehot = (regime[..., None] == levels).astype(jnp.float32)
    base_u = jnp.sum(onehot * regime_winds[:, 0], axis=-1)
    base_v = jnp.sum(onehot * regime_winds[:, 1], axis=-1)
    tile_u = base_u + 0.25 * (seeds % 13 - 6).astype(jnp.float32)
    tile_v = base_v + 0.4 * (seeds % 7 - 3).astype(jnp.float32)
    wind_u = jnp.repeat(jnp.repeat(tile_u, TILE_ROWS, axis=0), TILE_COLS, axis=1)
    wind_v = jnp.repeat(jnp.repeat(tile_v, TILE_ROWS, axis=0), TILE_COLS, axis=1)
    return (wind_u, wind_v)


def cell_terms(spectra, mixing, transfer, pattern, dissip):
    spectrum_shape = spectra.shape
    flattened = spectra.reshape(spectrum_shape[0], -1)
    mixed_terms = jnp.dot(mixing, flattened, preferred_element_type=jnp.float32)
    partner = jnp.take(flattened, pattern, axis=0)
    product = (mixed_terms * partner.astype(jnp.float32)).astype(jnp.bfloat16)
    nonlinear = jnp.dot(transfer, product, preferred_element_type=jnp.float32)
    widened = flattened.astype(jnp.float32)
    mean_energy = jnp.sum(widened, axis=0) / spectrum_shape[0]
    result = nonlinear - dissip[:, None] * mean_energy[None, :] * widened
    return result.astype(jnp.bfloat16).reshape(spectrum_shape)


def advect(padded, sea_field, courant_x, courant_y):
    flux_y = (
        jnp.maximum(courant_y, 0.0) * padded[..., :-1, :]
        + jnp.minimum(courant_y, 0.0) * padded[..., 1:, :]
    )
    center = padded[..., 1:-1, :]
    widths = [(0, 0)] * (center.ndim - 1) + [(1, 1)]
    padded_x = jnp.pad(center, widths)
    flux_x = (
        jnp.maximum(courant_x, 0.0) * padded_x[..., :-1]
        + jnp.minimum(courant_x, 0.0) * padded_x[..., 1:]
    )
    return (
        center - (flux_x[..., 1:] - flux_x[..., :-1]) - (flux_y[..., 1:, :] - flux_y[..., :-1, :])
    ) * sea_field


def per_device(
    energy,
    heading,
    growth,
    courant,
    dissip,
    mixing,
    transfer,
    pattern,
    regime_winds,
    regime,
    seeds,
    sea_mask,
):
    wind_u, wind_v = strip_winds(regime_winds, regime, seeds)
    widened = energy.astype(jnp.float32)
    drive = (
        wind_u[None] * jnp.cos(heading)[:, None, None]
        + wind_v[None] * jnp.sin(heading)[:, None, None]
    )
    input_term = growth[:, None, None] * jnp.maximum(0.0, drive) * widened
    returned = lax.all_to_all(
        cell_terms(
            lax.all_to_all(energy, "comp", split_axis=1, concat_axis=0, tiled=True),
            mixing,
            transfer,
            pattern,
            dissip,
        ),
        "comp",
        split_axis=0,
        concat_axis=1,
        tiled=True,
    )
    energy_field = widened + input_term + returned.astype(jnp.float32)
    sea_field = sea_mask.astype(jnp.float32)
    courant_x = courant[:, 0][:, None, None]
    courant_y = courant[:, 1][:, None, None]
    for substep in range(SUBSTEPS):
        padded = with_halo(energy_field, (("strip", 1),), 1)
        energy_field = advect(padded, sea_field, courant_x, courant_y)
    return energy_field

def exchange(value, axis, distance):
    count = lax.axis_size(axis)
    return lax.ppermute(value, axis, [(i, i ^ distance) for i in range(count)])


def spread_kernel(where, energy_ref, *refs):
    outs, wide = refs[:-1], refs[-1]
    group, rows, width = energy_ref.shape
    per_chip = rows // len(outs)
    for block in range(width // LANES):
        lanes = slice(block * LANES, (block + 1) * LANES)
        wide[block] = (
            energy_ref[:, :, lanes].astype(jnp.float32).reshape(group * rows, LANES)
        )
    for m, out_ref in enumerate(outs):
        first = per_chip * jnp.bitwise_xor(where[0], m)
        for row in range(per_chip):
            for block in range(width // LANES):
                start = row * width + block * LANES
                picked = wide[block, pl.ds(first + row, group, stride=rows), :]
                out_ref[:, start : start + LANES] = picked.astype(jnp.bfloat16)


def spread(where, energy, chips):
    local, rows, width = energy.shape
    cells = rows // chips * width
    block = 3 * GROUP
    return pl.pallas_call(
        spread_kernel,
        grid_spec=pltpu.PrefetchScalarGridSpec(
            num_scalar_prefetch=1,
            grid=(local // block,),
            in_specs=[pl.BlockSpec((block, rows, width), lambda i, w: (i, 0, 0))],
            out_specs=[pl.BlockSpec((block, cells), lambda i, w: (i, 0))] * chips,
            scratch_shapes=[pltpu.VMEM((width // LANES, block * rows, LANES), jnp.float32)],
        ),
        out_shape=[jax.ShapeDtypeStruct((local, cells), jnp.bfloat16)] * chips,
        compiler_params=pltpu.CompilerParams(vmem_limit_bytes=24 * MIB),
        cost_estimate=pl.CostEstimate(
            flops=energy.size, bytes_accessed=4 * energy.size, transcendentals=0
        ),
        name="spread",
    )(where, energy)


def weights_kernel(
    chips, where, column_ref, row_ref, mixing_ref, transfer_ref, first_ref, second_ref, pick, pick_t
):
    total = mixing_ref.shape[0]
    local = total // (2 * chips)
    tile = 384 if total % 384 == 0 else total
    pick[...] = (
        column_ref[...] == lax.broadcasted_iota(jnp.int32, (total, total), 1)
    ).astype(jnp.bfloat16)
    pick_t[...] = (
        row_ref[...] == lax.broadcasted_iota(jnp.int32, (total, total), 0)
    ).astype(jnp.bfloat16)

    for start in range(0, total, tile):
        first_ref[pl.ds(start, tile), :] = jnp.dot(
            pick_t[pl.ds(start, tile), :], mixing_ref[...], preferred_element_type=jnp.float32
        ).astype(jnp.bfloat16)
    extra = first_ref.shape[0] - total
    first_ref[pl.ds(total, extra), :] = jnp.ones((extra, total), jnp.bfloat16)
    for m in range(chips):
        block = 2 * jnp.bitwise_xor(where[0], m) + where[1]
        rows = transfer_ref[pl.ds(pl.multiple_of(block * local, GROUP), local), :]
        second_ref[pl.ds(m * local, local), :] = jnp.dot(
            rows, pick[...], preferred_element_type=jnp.float32
        ).astype(jnp.bfloat16)


def weights(where, pattern, mixing, transfer, chips):
    total = mixing.shape[0]
    whole = pl.BlockSpec(memory_space=pltpu.VMEM)
    return pl.pallas_call(
        functools.partial(weights_kernel, chips),
        in_specs=[pl.BlockSpec(memory_space=pltpu.SMEM)] + [whole] * 4,
        out_specs=[whole, whole],
        out_shape=[
            jax.ShapeDtypeStruct((total + GROUP, total), jnp.bfloat16),
            jax.ShapeDtypeStruct((total // 2, total), jnp.bfloat16),
        ],
        scratch_shapes=[pltpu.VMEM((total, total), jnp.bfloat16)] * 2,
        compiler_params=pltpu.CompilerParams(vmem_limit_bytes=32 * MIB),
        cost_estimate=pl.CostEstimate(
            flops=3 * total**3, bytes_accessed=8 * total**2, transcendentals=0
        ),
        name="weights",
    )(where, pattern[:, None], pattern[None, :], mixing, transfer)


def terms_kernel(chips, chunks, tile, where, first_ref, second_ref, dissip_ref, *refs):
    pieces = refs[: 2 * chips]
    outs = refs[2 * chips : -4]
    spectra, product, mixed, sems = refs[-4:]
    total, cells = spectra.shape
    local = total // (2 * chips)
    part = local // chunks

    def start_of(m, other):
        core = jnp.bitwise_xor(where[1], other)
        block = 2 * jnp.bitwise_xor(where[0], m) + core
        return pl.multiple_of(block * local, GROUP)

    copies = []
    for m in range(chips):
        for other in range(2):
            index = 2 * m + other
            copies.append(
                pltpu.make_async_copy(
                    pieces[m if other == 0 else chips + m],
                    spectra.at[pl.ds(start_of(m, other), local), :],
                    sems.at[index],
                )
            )
    for copy in copies:
        copy.start()
    for copy in copies:
        copy.wait()

    @pl.loop(0, cells // tile)
    def _(step):
        columns = pl.ds(pl.multiple_of(step * tile, tile), tile)
        mixed[...] = jnp.dot(
            first_ref[...], spectra[:, columns], preferred_element_type=jnp.float32
        )
        product[...] = (
            mixed[pl.ds(0, total), :] * spectra[:, columns].astype(jnp.float32)
        ).astype(jnp.bfloat16)
        mean = mixed[pl.ds(total, 1), :] * (1.0 / total)
        for m in range(chips):
            rows = pl.ds(start_of(m, 0), local)
            nonlinear = jnp.dot(
                second_ref[pl.ds(m * local, local), :],
                product[...],
                preferred_element_type=jnp.float32,
            )
            own = spectra[rows, columns].astype(jnp.float32)
            result = (nonlinear - dissip_ref[rows, :] * mean * own).astype(jnp.bfloat16)
            for j in range(chunks):
                outs[m * chunks + j][:, columns] = result[j * part : (j + 1) * part]


def source_terms(where, first, second, dissip, near, far, chunks):
    chips = len(near)
    local, cells = near[0].shape
    total = 2 * chips * local
    tile = 256
    whole = pl.BlockSpec(memory_space=pltpu.VMEM)
    outs = pl.pallas_call(
        functools.partial(terms_kernel, chips, chunks, tile),
        in_specs=[pl.BlockSpec(memory_space=pltpu.SMEM)]
        + [whole] * 3
        + [pl.BlockSpec(memory_space=pl.ANY)] * (2 * chips),
        out_specs=[whole] * (chips * chunks),
        out_shape=[jax.ShapeDtypeStruct((local // chunks, cells), jnp.bfloat16)]
        * (chips * chunks),
        scratch_shapes=[
            pltpu.VMEM((total, cells), jnp.bfloat16),
            pltpu.VMEM((total, tile), jnp.bfloat16),
            pltpu.VMEM((total + GROUP, tile), jnp.float32),
            pltpu.SemaphoreType.DMA((2 * chips,)),
        ],
        compiler_params=pltpu.CompilerParams(vmem_limit_bytes=32 * MIB),
        cost_estimate=pl.CostEstimate(
            flops=3 * total * total * cells, bytes_accessed=8 * total * cells, transcendentals=0
        ),
        name="source_terms",
    )(where, first, second, dissip[:, None], *near, *far)
    return [outs[m * chunks : (m + 1) * chunks] for m in range(chips)]


def propagate_kernel(chips, halo, where, coef_ref, wind_ref, mask_ref, *refs):
    count = chips + 2
    energies, terms = refs[:count], refs[count : 2 * count]
    out_ref, field, turned = refs[-3:]
    rows, group, width = field.shape
    inner = rows - 2 * halo
    per_chip = inner // chips

    def column(index):
        return jnp.broadcast_to(coef_ref[:, index : index + 1], (group, width))

    def force(energy_ref, term_ref, first, number):
        for row in range(number):
            here = first + row
            lanes = slice(row * width, (row + 1) * width)
            level = energy_ref[:, lanes].astype(jnp.float32)
            drive = (
                wind_ref[0, pl.ds(here, 1), :] * column(0)
                + wind_ref[1, pl.ds(here, 1), :] * column(1)
            )
            field[here] = level * (1.0 + jnp.maximum(drive, 0.0)) + term_ref[:, lanes].astype(
                jnp.float32
            )

    for m in range(chips):
        force(energies[m], terms[m], halo + per_chip * jnp.bitwise_xor(where[0], m), per_chip)
    force(energies[chips], terms[chips], 0, halo)
    force(energies[chips + 1], terms[chips + 1], halo + inner, halo)

    lane = lax.broadcasted_iota(jnp.int32, (group, width), 1)
    for substep in range(1, halo + 1):
        before = field[substep - 1]
        center = field[substep]
        for row in range(substep, rows - substep):
            after = field[row + 1]
            west = jnp.where(lane == 0, 0.0, pltpu.roll(center, 1, 1))
            east = jnp.where(lane == width - 1, 0.0, pltpu.roll(center, width - 1, 1))
            value = (
                center * column(2)
                + west * column(3)
                + east * column(4)
                + before * column(5)
                + after * column(6)
            ) * mask_ref[pl.ds(row, 1), :]
            if substep < halo:
                field[row] = value
            else:
                for block in range(width // LANES):
                    lanes = slice(block * LANES, (block + 1) * LANES)
                    turned[block, pl.ds(row - halo, group, stride=inner), :] = value[:, lanes]
            before, center = center, after
    for block in range(width // LANES):
        out_ref[:, block * LANES : (block + 1) * LANES] = turned[block]


def propagate(where, coef, winds, mask, energies, terms, chunk, chunks, previous, halo):
    chips = len(energies) - 2
    local = energies[0].shape[0]
    rows, width = mask.shape
    inner = rows - 2 * halo
    steps = local // chunks // GROUP
    base = chunk * steps
    cells, edge = energies[0].shape[1], energies[-1].shape[1]
    shape = jax.ShapeDtypeStruct((local * inner, width), jnp.float32)
    in_specs = (
        [
            pl.BlockSpec((GROUP, coef.shape[1]), lambda i, w: (base + i, 0)),
            pl.BlockSpec(winds.shape, lambda i, w: (0, 0, 0)),
            pl.BlockSpec(mask.shape, lambda i, w: (0, 0)),
        ]
        + [pl.BlockSpec((GROUP, cells), lambda i, w: (base + i, 0))] * chips
        + [pl.BlockSpec((GROUP, edge), lambda i, w: (base + i, 0))] * 2
        + [pl.BlockSpec((GROUP, cells), lambda i, w: (i, 0))] * chips
        + [pl.BlockSpec((GROUP, edge), lambda i, w: (i, 0))] * 2
    )
    operands = [where, coef, winds, mask, *energies, *terms]
    aliases = {}
    kernel = functools.partial(propagate_kernel, chips, halo)
    if previous is not None:
        aliases = {len(operands): 0}
        operands.append(previous)
        in_specs.append(pl.BlockSpec(memory_space=pl.ANY))
    return pl.pallas_call(
        kernel,
        grid_spec=pltpu.PrefetchScalarGridSpec(
            num_scalar_prefetch=1,
            grid=(steps,),
            in_specs=in_specs,
            out_specs=pl.BlockSpec((GROUP * inner, width), lambda i, w: (base + i, 0)),
            scratch_shapes=[
                pltpu.VMEM((rows, GROUP, width), jnp.float32),
                pltpu.VMEM((width // LANES, GROUP * inner, LANES), jnp.float32),
            ],
        ),
        out_shape=shape,
        input_output_aliases=aliases,
        compiler_params=pltpu.CompilerParams(vmem_limit_bytes=24 * MIB),
        cost_estimate=pl.CostEstimate(
            flops=60 * shape.size // chunks,
            bytes_accessed=8 * shape.size // chunks,
            transcendentals=0,
        ),
        name="propagate",
    )(*operands)


def chosen(values, index):
    result = values[0]
    for m in range(1, len(values)):
        result = jnp.where(index == m, values[m], result)
    return result


def from_below(value):
    count = lax.axis_size("strip")
    return lax.ppermute(value, "strip", [(i, i + 1) for i in range(count - 1)])


def from_above(value):
    count = lax.axis_size("strip")
    return lax.ppermute(value, "strip", [(i + 1, i) for i in range(count - 1)])


def per_device_paired(
    energy,
    heading,
    growth,
    courant,
    dissip,
    mixing,
    transfer,
    pattern,
    regime_winds,
    regime,
    seeds,
    sea_mask,
):
    chips = lax.axis_size("comp") // 2
    chunks = 3
    local, rows, width = energy.shape
    halo = SUBSTEPS
    me = lax.axis_index("comp")
    chip = me // 2
    where = jnp.stack([chip, me % 2]).astype(jnp.int32)

    spread_out = spread(where, energy, chips)
    near = [spread_out[0]] + [exchange(spread_out[m], "comp", 2 * m) for m in range(1, chips)]
    far = [exchange(value, "comp", 1) for value in near]

    first, second = weights(where, pattern, mixing, transfer, chips)

    wind_u, wind_v = strip_winds(regime_winds, regime, seeds)
    fields = jnp.stack([wind_u, wind_v, sea_mask.astype(jnp.float32)])
    fields = jnp.concatenate(
        [from_below(fields[:, rows - halo :]), fields, from_above(fields[:, :halo])], axis=1
    )
    top, bottom = jnp.bitwise_xor(chip, chips - 1), chip
    energies = list(spread_out) + [
        from_below(chosen(spread_out, top)),
        from_above(chosen(spread_out, bottom)),
    ]
    along, across = courant[:, 0], courant[:, 1]
    coef = jnp.stack(
        [
            growth * jnp.cos(heading),
            growth * jnp.sin(heading),
            1.0 - jnp.abs(along) - jnp.abs(across),
            jnp.maximum(along, 0.0),
            -jnp.minimum(along, 0.0),
            jnp.maximum(across, 0.0),
            -jnp.minimum(across, 0.0),
            jnp.zeros_like(along),
        ],
        axis=1,
    )

    sent = source_terms(where, first, second, dissip, near, far, chunks)
    result = None
    for j in range(chunks):
        terms = [sent[0][j]] + [exchange(sent[m][j], "comp", 2 * m) for m in range(1, chips)]
        terms = terms + [from_below(chosen(terms, top)), from_above(chosen(terms, bottom))]
        result = propagate(
            where, coef, fields[:2], fields[2], energies, terms, j, chunks, result, halo
        )
    return result.reshape(local, rows, width)


def solution(mesh):
    placed = (
        P("comp", "strip", None),
        P("comp"),
        P("comp"),
        P("comp", None),
        P(),
        P(),
        P(),
        P(),
        P(),
        P("strip", None),
        P("strip", None),
        P("strip", None),
    )
    paired = mesh.shape["comp"] == 8
    body = per_device_paired if paired else per_device
    return jax.shard_map(
        body, mesh=mesh, in_specs=placed, out_specs=P("comp", "strip", None), check_vma=False
    )
```

```python
import functools
import jax
import jax.numpy as jnp
from jax import lax
from jax.experimental import pallas as pl
from jax.experimental.pallas import tpu as pltpu
from jax.sharding import PartitionSpec as P

SUBSTEPS = 4
TILE_ROWS = 2
TILE_COLS = 16
GROUP = 16
SUBLANES = 8
LANES = 128
MIB = 1 << 20


def with_halo(block, sides, width):
    for axis, dim in sides:
        count = lax.axis_size(axis)
        forward = [(i, i + 1) for i in range(count - 1)]
        backward = [(target, source) for source, target in forward]
        low = lax.ppermute(
            lax.slice_in_dim(block, block.shape[dim] - width, None, axis=dim), axis, forward
        )
        high = lax.ppermute(lax.slice_in_dim(block, 0, width, axis=dim), axis, backward)
        block = jnp.concatenate([low, block, high], axis=dim)
    return block


def strip_winds(regime_winds, regime, seeds):
    levels = jnp.arange(regime_winds.shape[0], dtype=jnp.int32)
    onehot = (regime[..., None] == levels).astype(jnp.float32)
    base_u = jnp.sum(onehot * regime_winds[:, 0], axis=-1)
    base_v = jnp.sum(onehot * regime_winds[:, 1], axis=-1)
    tile_u = base_u + 0.25 * (seeds % 13 - 6).astype(jnp.float32)
    tile_v = base_v + 0.4 * (seeds % 7 - 3).astype(jnp.float32)
    wind_u = jnp.repeat(jnp.repeat(tile_u, TILE_ROWS, axis=0), TILE_COLS, axis=1)
    wind_v = jnp.repeat(jnp.repeat(tile_v, TILE_ROWS, axis=0), TILE_COLS, axis=1)
    return (wind_u, wind_v)


def cell_terms(spectra, mixing, transfer, pattern, dissip):
    spectrum_shape = spectra.shape
    flattened = spectra.reshape(spectrum_shape[0], -1)
    mixed_terms = jnp.dot(mixing, flattened, preferred_element_type=jnp.float32)
    partner = jnp.take(flattened, pattern, axis=0)
    product = (mixed_terms * partner.astype(jnp.float32)).astype(jnp.bfloat16)
    nonlinear = jnp.dot(transfer, product, preferred_element_type=jnp.float32)
    widened = flattened.astype(jnp.float32)
    mean_energy = jnp.sum(widened, axis=0) / spectrum_shape[0]
    result = nonlinear - dissip[:, None] * mean_energy[None, :] * widened
    return result.astype(jnp.bfloat16).reshape(spectrum_shape)


def advect(padded, sea_field, courant_x, courant_y):
    flux_y = (
        jnp.maximum(courant_y, 0.0) * padded[..., :-1, :]
        + jnp.minimum(courant_y, 0.0) * padded[..., 1:, :]
    )
    center = padded[..., 1:-1, :]
    widths = [(0, 0)] * (center.ndim - 1) + [(1, 1)]
    padded_x = jnp.pad(center, widths)
    flux_x = (
        jnp.maximum(courant_x, 0.0) * padded_x[..., :-1]
        + jnp.minimum(courant_x, 0.0) * padded_x[..., 1:]
    )
    return (
        center - (flux_x[..., 1:] - flux_x[..., :-1]) - (flux_y[..., 1:, :] - flux_y[..., :-1, :])
    ) * sea_field


def per_device(
    energy,
    heading,
    growth,
    courant,
    dissip,
    mixing,
    transfer,
    pattern,
    regime_winds,
    regime,
    seeds,
    sea_mask,
):
    wind_u, wind_v = strip_winds(regime_winds, regime, seeds)
    widened = energy.astype(jnp.float32)
    drive = (
        wind_u[None] * jnp.cos(heading)[:, None, None]
        + wind_v[None] * jnp.sin(heading)[:, None, None]
    )
    input_term = growth[:, None, None] * jnp.maximum(0.0, drive) * widened
    returned = lax.all_to_all(
        cell_terms(
            lax.all_to_all(energy, "comp", split_axis=1, concat_axis=0, tiled=True),
            mixing,
            transfer,
            pattern,
            dissip,
        ),
        "comp",
        split_axis=0,
        concat_axis=1,
        tiled=True,
    )
    energy_field = widened + input_term + returned.astype(jnp.float32)
    sea_field = sea_mask.astype(jnp.float32)
    courant_x = courant[:, 0][:, None, None]
    courant_y = courant[:, 1][:, None, None]
    for substep in range(SUBSTEPS):
        padded = with_halo(energy_field, (("strip", 1),), 1)
        energy_field = advect(padded, sea_field, courant_x, courant_y)
    return energy_field

def exchange(value, axis, distance):
    count = lax.axis_size(axis)
    return lax.ppermute(value, axis, [(i, i ^ distance) for i in range(count)])


def in_hbm(value):
    return pltpu.with_memory_space_constraint(value, pltpu.MemorySpace.HBM)


def spread_kernel(chips, halo, where, energy_ref, *refs):
    outs, wide = refs[:-1], refs[-1]
    group, rows, width = energy_ref.shape
    for block in range(width // LANES):
        lanes = slice(block * LANES, (block + 1) * LANES)
        wide[block] = (
            energy_ref[:, :, lanes].astype(jnp.float32).reshape(group * rows, LANES)
        )

    def place(out_ref, slot, row):
        for block in range(width // LANES):
            start = slot * width + block * LANES
            picked = wide[block, pl.ds(row, group, stride=rows), :]
            out_ref[:, start : start + LANES] = picked.astype(jnp.bfloat16)

    for m in range(chips):
        chip = jnp.bitwise_xor(where[0], m)
        for slot in range(2):
            place(outs[m], slot, chip + slot * (rows - halo))
            place(outs[chips + m], slot, chip + (slot + 1) * halo)
        for side in range(2):
            place(outs[2 * chips + side], m, chip + (rows - halo) * where[2 + side])


def spread(where, energy, chips, halo):
    local, rows, width = energy.shape
    block = 3 * GROUP
    sizes = [2 * width] * (2 * chips) + [halo * width] * 2
    return pl.pallas_call(
        functools.partial(spread_kernel, chips, halo),
        grid_spec=pltpu.PrefetchScalarGridSpec(
            num_scalar_prefetch=1,
            grid=(local // block,),
            in_specs=[pl.BlockSpec((block, rows, width), lambda i, w: (i, 0, 0))],
            out_specs=[pl.BlockSpec((block, size), lambda i, w: (i, 0)) for size in sizes],
            scratch_shapes=[pltpu.VMEM((width // LANES, block * rows, LANES), jnp.float32)],
        ),
        out_shape=[pltpu.MemorySpace.HBM((local, size), jnp.bfloat16) for size in sizes],
        compiler_params=pltpu.CompilerParams(vmem_limit_bytes=12 * MIB),
        cost_estimate=pl.CostEstimate(
            flops=energy.size, bytes_accessed=4 * energy.size, transcendentals=0
        ),
        name="spread",
    )(where, energy)


def gather_kernel(chips, parts, where, extra_ref, *refs):
    pieces, outs, sems = refs[:chips], refs[chips:-1], refs[-1]
    width = pieces[0].shape[1] // 2
    copies = []
    for side in range(2):
        start = pl.multiple_of(width * where[2 + side], LANES)
        begin = 0
        for index, part in enumerate(parts):
            out = outs[2 * index + side]
            for m in range(chips):
                copies.append(
                    pltpu.make_async_copy(
                        pieces[m].at[begin : begin + part, pl.ds(start, width)],
                        out.at[:part, m * width : (m + 1) * width],
                        sems.at[len(copies)],
                    )
                )
            if index == 0:
                out[part:, :] = extra_ref[side]
            begin += part
    for copy in copies:
        copy.start()
    for copy in copies:
        copy.wait()


def gather_edges(where, extra, landed, parts):
    chips = len(landed)
    width = landed[0].shape[1] // 2
    shapes = [part + (GROUP if index == 0 else 0) for index, part in enumerate(parts)]
    whole = pl.BlockSpec(memory_space=pltpu.VMEM)
    return pl.pallas_call(
        functools.partial(gather_kernel, chips, parts),
        in_specs=[pl.BlockSpec(memory_space=pltpu.SMEM), whole]
        + [pl.BlockSpec(memory_space=pl.ANY)] * chips,
        out_specs=[whole] * (2 * len(parts)),
        out_shape=[
            jax.ShapeDtypeStruct((shape, chips * width), jnp.bfloat16)
            for shape in shapes
            for side in range(2)
        ],
        scratch_shapes=[pltpu.SemaphoreType.DMA((2 * chips * len(parts),))],
        compiler_params=pltpu.CompilerParams(vmem_limit_bytes=4 * MIB),
        cost_estimate=pl.CostEstimate(
            flops=0, bytes_accessed=4 * chips * sum(shapes) * width, transcendentals=0
        ),
        name="gather_edges",
    )(where, extra, *landed)


def weights_kernel(
    chips,
    where,
    column_ref,
    row_ref,
    mixing_hbm,
    transfer_hbm,
    first_hbm,
    second_hbm,
    pick,
    mixing_ref,
    transfer_ref,
    first_ref,
    second_ref,
    in_sems,
    out_sems,
):
    total = mixing_ref.shape[0]
    local = total // (2 * chips)
    stripe = total // chips
    loads = [
        pltpu.make_async_copy(mixing_hbm, mixing_ref, in_sems.at[0]),
        pltpu.make_async_copy(transfer_hbm, transfer_ref, in_sems.at[1]),
    ]
    for load in loads:
        load.start()
    pick[...] = (
        column_ref[...] == lax.broadcasted_iota(jnp.int32, (total, total), 1)
    ).astype(jnp.bfloat16)
    extra = first_ref.shape[0] - total
    first_ref[total:, :] = jnp.ones((extra, total), jnp.bfloat16)
    stores = []

    def send(source, target, start, size):
        store = pltpu.make_async_copy(
            source.at[start : start + size, :],
            target.at[start : start + size, :],
            out_sems.at[len(stores)],
        )
        store.start()
        stores.append(store)

    for load in loads:
        load.wait()
    for start in range(0, total, stripe):
        rows = lax.broadcasted_iota(jnp.int32, (stripe, total), 0) + start
        chosen = (row_ref[...] == rows).astype(jnp.bfloat16)
        first_ref[start : start + stripe, :] = jnp.dot(
            chosen, mixing_ref[...], preferred_element_type=jnp.float32
        ).astype(jnp.bfloat16)
        send(first_ref, first_hbm, start, stripe + (extra if start + stripe == total else 0))
    for m in range(chips):
        block = 2 * jnp.bitwise_xor(where[0], m) + where[1]
        rows = transfer_ref[pl.ds(pl.multiple_of(block * local, GROUP), local), :]
        second_ref[m * local : (m + 1) * local, :] = jnp.dot(
            rows, pick[...], preferred_element_type=jnp.float32
        ).astype(jnp.bfloat16)
        send(second_ref, second_hbm, m * local, local)
    for store in stores:
        store.wait()


def weights(where, pattern, mixing, transfer, chips):
    total = mixing.shape[0]
    whole = pl.BlockSpec(memory_space=pltpu.VMEM)
    outside = pl.BlockSpec(memory_space=pltpu.MemorySpace.HBM)
    shapes = [(total + GROUP, total), (total // 2, total)]
    return pl.pallas_call(
        functools.partial(weights_kernel, chips),
        in_specs=[pl.BlockSpec(memory_space=pltpu.SMEM)] + [whole] * 2 + [outside] * 2,
        out_specs=[outside] * 2,
        out_shape=[pltpu.MemorySpace.HBM(shape, jnp.bfloat16) for shape in shapes],
        scratch_shapes=[pltpu.VMEM((total, total), jnp.bfloat16)] * 3
        + [pltpu.VMEM(shape, jnp.bfloat16) for shape in shapes]
        + [pltpu.SemaphoreType.DMA((2,)), pltpu.SemaphoreType.DMA((2 * chips,))],
        compiler_params=pltpu.CompilerParams(vmem_limit_bytes=20 * MIB),
        cost_estimate=pl.CostEstimate(
            flops=3 * total**3, bytes_accessed=8 * total**2, transcendentals=0
        ),
        name="weights",
    )(where, pattern[:, None], pattern[None, :], in_hbm(mixing), in_hbm(transfer))


def terms_kernel(chips, where, dissip_ref, first_hbm, second_hbm, *refs):
    pieces, outs = refs[: 2 * chips], refs[2 * chips : 3 * chips]
    spectra, product, result, first_ref, second_ref, in_sems, weight_sems, out_sems = refs[
        3 * chips :
    ]
    total = spectra.shape[0]
    local = total // (2 * chips)
    stripe = total // chips
    extra = first_ref.shape[0] - total

    def start_of(m, other):
        core = jnp.bitwise_xor(where[1], other)
        block = 2 * jnp.bitwise_xor(where[0], m) + core
        return pl.multiple_of(block * local, GROUP)

    copies = [
        pltpu.make_async_copy(
            pieces[m + other * chips],
            spectra.at[pl.ds(start_of(m, other), local), :],
            in_sems.at[2 * m + other],
        )
        for m in range(chips)
        for other in range(2)
    ]
    stripes = []
    for index in range(chips):
        begin = index * stripe
        end = begin + stripe + (extra if index == chips - 1 else 0)
        stripes.append(
            pltpu.make_async_copy(
                first_hbm.at[begin:end, :], first_ref.at[begin:end, :], weight_sems.at[index]
            )
        )
    load = pltpu.make_async_copy(second_hbm, second_ref, weight_sems.at[chips])
    for copy in [*copies, *stripes, load]:
        copy.start()
    for copy in copies:
        copy.wait()

    for index in range(chips):
        start = index * stripe
        last = index == chips - 1
        stripes[index].wait()
        mixed = jnp.dot(
            first_ref[start : start + stripe + (extra if last else 0), :],
            spectra[...],
            preferred_element_type=jnp.float32,
        )
        product[start : start + stripe, :] = (
            mixed[:stripe] * spectra[start : start + stripe, :].astype(jnp.float32)
        ).astype(jnp.bfloat16)
        if last:
            mean = mixed[stripe : stripe + 1] * (1.0 / total)
    load.wait()
    sent = []
    for m in range(chips):
        rows = pl.ds(start_of(m, 0), local)
        mine = slice(m * local, (m + 1) * local)
        nonlinear = jnp.dot(
            second_ref[mine, :], product[...], preferred_element_type=jnp.float32
        )
        own = spectra[rows, :].astype(jnp.float32)
        result[mine, :] = (nonlinear - dissip_ref[rows, :] * mean * own).astype(jnp.bfloat16)
        copy = pltpu.make_async_copy(result.at[mine, :], outs[m], out_sems.at[m])
        copy.start()
        sent.append(copy)
    for copy in sent:
        copy.wait()


def source_terms(where, first, second, dissip, near, far):
    chips = len(near)
    local, cells = near[0].shape
    total = 2 * chips * local
    outside = pl.BlockSpec(memory_space=pltpu.MemorySpace.HBM)
    return pl.pallas_call(
        functools.partial(terms_kernel, chips),
        in_specs=[
            pl.BlockSpec(memory_space=pltpu.SMEM),
            pl.BlockSpec(memory_space=pltpu.VMEM),
            outside,
            outside,
        ]
        + [pl.BlockSpec(memory_space=pl.ANY)] * (2 * chips),
        out_specs=[outside] * chips,
        out_shape=[pltpu.MemorySpace.HBM((local, cells), jnp.bfloat16)] * chips,
        scratch_shapes=[
            pltpu.VMEM((total, cells), jnp.bfloat16),
            pltpu.VMEM((total, cells), jnp.bfloat16),
            pltpu.VMEM((total // 2, cells), jnp.bfloat16),
            pltpu.VMEM(first.shape, jnp.bfloat16),
            pltpu.VMEM(second.shape, jnp.bfloat16),
            pltpu.SemaphoreType.DMA((2 * chips,)),
            pltpu.SemaphoreType.DMA((chips + 1,)),
            pltpu.SemaphoreType.DMA((chips,)),
        ],
        compiler_params=pltpu.CompilerParams(vmem_limit_bytes=18 * MIB),
        cost_estimate=pl.CostEstimate(
            flops=3 * total * total * cells, bytes_accessed=8 * total * cells, transcendentals=0
        ),
        name="source_terms",
    )(where, dissip[:, None], in_hbm(first), in_hbm(second), *near, *far)


def propagate_kernel(chips, halo, where, coef_ref, fields_ref, *refs):
    count = 2 * chips + 2
    energies, edges, terms = refs[:count], refs[count : count + 2], refs[count + 2 : 2 * count + 2]
    out_ref, field, turned, weather = refs[-4:]
    rows, blocks, group, lanes = field.shape
    width = blocks * lanes
    inner = rows - 2 * halo

    def column(at, number, index):
        return jnp.broadcast_to(coef_ref[at : at + number, index : index + 1], (number, lanes))

    cosine, sine = column(0, group, 0), column(0, group, 1)

    firsts = [(halo + inner) * where[2 + side] for side in range(2)]

    @pl.when(pl.program_id(0) == 0)
    def _():
        for index in range(3):
            for row in range(inner):
                for b in range(blocks):
                    part = slice(b * lanes, (b + 1) * lanes)
                    weather[index, halo + row, b] = jnp.broadcast_to(
                        fields_ref[index, row : row + 1, part], (SUBLANES, lanes)
                    )
        for side in range(2):
            pieces = edges[side][...].astype(jnp.float32)
            for index in range(3):
                value = pieces[3 * index : 3 * index + 1]
                value = value + pieces[3 * index + 1 : 3 * index + 2]
                value = value + pieces[3 * index + 2 : 3 * index + 3]
                value = jnp.where(where[4 + side] == 1, value, 0.0)
                for row in range(halo):
                    for b in range(blocks):
                        at = row * width + b * lanes
                        weather[index, firsts[side] + row, b] = jnp.broadcast_to(
                            value[:, at : at + lanes], (SUBLANES, lanes)
                        )

    def force(energy_ref, term_ref, slot, row, valid=None):
        for b in range(blocks):
            at = slice(slot * width + b * lanes, slot * width + (b + 1) * lanes)
            wind_u = jnp.concatenate([weather[0, row, b]] * (group // SUBLANES))
            wind_v = jnp.concatenate([weather[1, row, b]] * (group // SUBLANES))
            drive = wind_u * cosine + wind_v * sine
            value = energy_ref[:, at].astype(jnp.float32) * (
                1.0 + jnp.maximum(drive, 0.0)
            ) + term_ref[:, at].astype(jnp.float32)
            if valid is not None:
                value = jnp.where(valid == 1, value, 0.0)
            field[row, b] = value

    for m in range(chips):
        chip = jnp.bitwise_xor(where[0], m)
        for slot in range(2):
            force(energies[m], terms[m], slot, halo + chip + slot * (inner - halo))
            force(energies[chips + m], terms[chips + m], slot, halo + chip + (slot + 1) * halo)
        for side in range(2):
            index = 2 * chips + side
            force(energies[index], terms[index], m, firsts[side] + chip, where[4 + side])

    lane = lax.broadcasted_iota(jnp.int32, (SUBLANES, lanes), 1)
    for at in range(0, group, SUBLANES):
        here = slice(at, at + SUBLANES)
        keep, west, east, south, north = [column(at, SUBLANES, i) for i in range(2, 7)]
        from_west, from_south = west > 0.0, south > 0.0
        source = jnp.bitwise_and(jnp.where(from_west, lane - 1, lane + 1), lanes - 1)
        first_lane = jnp.logical_and(from_west, lane == 0)
        last_lane = jnp.logical_and(jnp.logical_not(from_west), lane == lanes - 1)
        along, across = west + east, south + north
        for substep in range(1, halo + 1):
            before = [field[substep - 1, b, here] for b in range(blocks)]
            center = [field[substep, b, here] for b in range(blocks)]
            for row in range(substep, rows - substep):
                after = [field[row + 1, b, here] for b in range(blocks)]
                moved = [jnp.take_along_axis(value, source, axis=1) for value in center]
                for b in range(blocks):
                    beside = jnp.where(first_lane, moved[b - 1] if b > 0 else 0.0, moved[b])
                    beside = jnp.where(
                        last_lane, moved[b + 1] if b < blocks - 1 else 0.0, beside
                    )
                    upwind = jnp.where(from_south, before[b], after[b])
                    value = (center[b] * keep + beside * along + upwind * across) * weather[
                        2, row, b
                    ]
                    if substep < halo:
                        field[row, b, here] = value
                    else:
                        turned[
                            b, pl.ds(at * inner + row - halo, SUBLANES, stride=inner), :
                        ] = value
                before, center = center, after
    for b in range(blocks):
        out_ref[:, b * lanes : (b + 1) * lanes] = turned[b]


def propagate(where, coef, fields, energies, edges, terms, begin, part, previous, halo):
    chips = (len(energies) - 2) // 2
    local = energies[0].shape[0]
    inner, width = fields.shape[1:]
    rows = inner + 2 * halo
    steps = part // GROUP
    base = begin // GROUP
    last = edges[0].shape[0] // GROUP - 1
    cells, edge = energies[0].shape[1], energies[-1].shape[1]
    shape = jax.ShapeDtypeStruct((local * inner, width), jnp.float32)
    at_base = lambda i, w: (base + i, 0)
    in_specs = (
        [
            pl.BlockSpec((GROUP, coef.shape[1]), at_base),
            pl.BlockSpec(fields.shape, lambda i, w: (0, 0, 0)),
        ]
        + [pl.BlockSpec((GROUP, cells), at_base)] * (2 * chips)
        + [pl.BlockSpec((GROUP, edge), at_base)] * 2
        + [pl.BlockSpec((GROUP, edge), lambda i, w: (last, 0))] * 2
        + [pl.BlockSpec((GROUP, cells), at_base)] * (2 * chips)
        + [pl.BlockSpec((GROUP, edge), lambda i, w: (i, 0))] * 2
    )
    operands = [where, coef, fields, *map(in_hbm, energies), *edges]
    operands += [*map(in_hbm, terms[: 2 * chips]), *terms[2 * chips :]]
    aliases = {}
    kernel = functools.partial(propagate_kernel, chips, halo)
    if previous is not None:
        aliases = {len(operands): 0}
        operands.append(previous)
        in_specs.append(pl.BlockSpec(memory_space=pl.ANY))
    return pl.pallas_call(
        kernel,
        grid_spec=pltpu.PrefetchScalarGridSpec(
            num_scalar_prefetch=1,
            grid=(steps,),
            in_specs=in_specs,
            out_specs=pl.BlockSpec((GROUP * inner, width), lambda i, w: (base + i, 0)),
            scratch_shapes=[
                pltpu.VMEM((rows, width // LANES, GROUP, LANES), jnp.float32),
                pltpu.VMEM((width // LANES, GROUP * inner, LANES), jnp.float32),
                pltpu.VMEM((3, rows, width // LANES, SUBLANES, LANES), jnp.float32),
            ],
        ),
        out_shape=shape,
        input_output_aliases=aliases,
        compiler_params=pltpu.CompilerParams(vmem_limit_bytes=10 * MIB),
        cost_estimate=pl.CostEstimate(
            flops=60 * shape.size * part // local,
            bytes_accessed=8 * shape.size * part // local,
            transcendentals=0,
        ),
        name="propagate",
    )(*operands)


def thirds(value):
    pieces, rest = [], value
    for _ in range(3):
        piece = lax.reduce_precision(rest, 8, 7)
        pieces.append(piece)
        rest = rest - piece
    stacked = jnp.stack(pieces, axis=1).reshape(3 * value.shape[0], value.shape[1])
    return jnp.pad(stacked, ((0, GROUP - stacked.shape[0]), (0, 0))).astype(jnp.bfloat16)


def pair_up(value, start):
    count = lax.axis_size("strip")
    target = list(range(count))
    for i in range(start, count - 1, 2):
        target[i], target[i + 1] = i + 1, i
    return lax.ppermute(value, "strip", list(enumerate(target)))


def per_device_paired(
    energy,
    heading,
    growth,
    courant,
    dissip,
    mixing,
    transfer,
    pattern,
    regime_winds,
    regime,
    seeds,
    sea_mask,
):
    chips = lax.axis_size("comp") // 2
    local, rows, width = energy.shape
    halo = SUBSTEPS
    units = local // GROUP
    parts = (units // 2 * GROUP, (units - units // 2) * GROUP)
    me, strip, strips = lax.axis_index("comp"), lax.axis_index("strip"), lax.axis_size("strip")
    chip, odd = me // 2, strip % 2
    has_above = (strip > 0).astype(jnp.int32)
    has_below = (strip < strips - 1).astype(jnp.int32)
    where = jnp.stack(
        [
            chip,
            me % 2,
            1 - odd,
            odd,
            jnp.where(odd == 1, has_above, has_below),
            jnp.where(odd == 1, has_below, has_above),
        ]
    ).astype(jnp.int32)

    pieces = spread(where, energy, chips, halo)
    outer, rest = pieces[:chips], pieces[chips:]
    near_outer = [outer[0]] + [exchange(outer[m], "comp", 2 * m) for m in range(1, chips)]
    first, second = weights(where, pattern, mixing, transfer, chips)
    near_outer, rest, first, second = lax.optimization_barrier(
        (near_outer, rest, first, second)
    )
    middle, sides = rest[:chips], rest[chips:]
    near_middle = [middle[0]] + [exchange(middle[m], "comp", 2 * m) for m in range(1, chips)]
    energies = [*outer, *middle] + [pair_up(sides[side], side) for side in range(2)]

    far_outer = [exchange(value, "comp", 1) for value in near_outer]
    sent_outer = source_terms(where, first, second, dissip, near_outer, far_outer)
    landed_outer = [sent_outer[0]] + [
        exchange(sent_outer[m], "comp", 2 * m) for m in range(1, chips)
    ]

    wind_u, wind_v = strip_winds(regime_winds, regime, seeds)
    fields = jnp.stack([wind_u, wind_v, sea_mask.astype(jnp.float32)])
    upper, lower = fields[:, :halo], fields[:, rows - halo :]
    extra = jnp.stack(
        [
            thirds(jnp.where(odd == 1, upper, lower).reshape(3, -1)),
            thirds(jnp.where(odd == 1, lower, upper).reshape(3, -1)),
        ]
    )
    along, across = courant[:, 0], courant[:, 1]
    coef = jnp.stack(
        [
            growth * jnp.cos(heading),
            growth * jnp.sin(heading),
            1.0 - jnp.abs(along) - jnp.abs(across),
            jnp.maximum(along, 0.0),
            -jnp.minimum(along, 0.0),
            jnp.maximum(across, 0.0),
            -jnp.minimum(across, 0.0),
            jnp.zeros_like(along),
        ],
        axis=1,
    )

    near_middle, sent_outer = lax.optimization_barrier((near_middle, sent_outer))
    far_middle = [exchange(value, "comp", 1) for value in near_middle]
    sent_middle = source_terms(where, first, second, dissip, near_middle, far_middle)
    landed_middle = [sent_middle[0]] + [
        exchange(sent_middle[m], "comp", 2 * m) for m in range(1, chips)
    ]

    edges = gather_edges(where, extra, landed_outer, parts)
    edges = [pair_up(edge, index % 2) for index, edge in enumerate(edges)]
    landed = [*landed_outer, *landed_middle]
    result = None
    for j in range(len(parts)):
        result = propagate(
            where,
            coef,
            fields,
            energies,
            edges[:2],
            landed + edges[2 * j : 2 * j + 2],
            sum(parts[:j]),
            parts[j],
            result,
            halo,
        )
    return result.reshape(local, rows, width)


def solution(mesh):
    placed = (
        P("comp", "strip", None),
        P("comp"),
        P("comp"),
        P("comp", None),
        P(),
        P(),
        P(),
        P(),
        P(),
        P("strip", None),
        P("strip", None),
        P("strip", None),
    )
    paired = mesh.shape["comp"] == 2 * SUBSTEPS
    body = per_device_paired if paired else per_device
    return jax.shard_map(
        body, mesh=mesh, in_specs=placed, out_specs=P("comp", "strip", None), check_vma=False
    )
```

```python
import functools
import jax
import jax.numpy as jnp
from jax import lax
from jax.experimental import pallas as pl
from jax.experimental.pallas import tpu as pltpu
from jax.sharding import PartitionSpec as P

SUBSTEPS = 4
TILE_ROWS = 2
TILE_COLS = 16
GROUP = 16
SUBLANES = 8
LANES = 128
MIB = 1 << 20


def with_halo(block, sides, width):
    for axis, dim in sides:
        count = lax.axis_size(axis)
        forward = [(i, i + 1) for i in range(count - 1)]
        backward = [(target, source) for source, target in forward]
        low = lax.ppermute(
            lax.slice_in_dim(block, block.shape[dim] - width, None, axis=dim), axis, forward
        )
        high = lax.ppermute(lax.slice_in_dim(block, 0, width, axis=dim), axis, backward)
        block = jnp.concatenate([low, block, high], axis=dim)
    return block


def strip_winds(regime_winds, regime, seeds):
    levels = jnp.arange(regime_winds.shape[0], dtype=jnp.int32)
    onehot = (regime[..., None] == levels).astype(jnp.float32)
    base_u = jnp.sum(onehot * regime_winds[:, 0], axis=-1)
    base_v = jnp.sum(onehot * regime_winds[:, 1], axis=-1)
    tile_u = base_u + 0.25 * (seeds % 13 - 6).astype(jnp.float32)
    tile_v = base_v + 0.4 * (seeds % 7 - 3).astype(jnp.float32)
    wind_u = jnp.repeat(jnp.repeat(tile_u, TILE_ROWS, axis=0), TILE_COLS, axis=1)
    wind_v = jnp.repeat(jnp.repeat(tile_v, TILE_ROWS, axis=0), TILE_COLS, axis=1)
    return (wind_u, wind_v)


def cell_terms(spectra, mixing, transfer, pattern, dissip):
    spectrum_shape = spectra.shape
    flattened = spectra.reshape(spectrum_shape[0], -1)
    mixed_terms = jnp.dot(mixing, flattened, preferred_element_type=jnp.float32)
    partner = jnp.take(flattened, pattern, axis=0)
    product = (mixed_terms * partner.astype(jnp.float32)).astype(jnp.bfloat16)
    nonlinear = jnp.dot(transfer, product, preferred_element_type=jnp.float32)
    widened = flattened.astype(jnp.float32)
    mean_energy = jnp.sum(widened, axis=0) / spectrum_shape[0]
    result = nonlinear - dissip[:, None] * mean_energy[None, :] * widened
    return result.astype(jnp.bfloat16).reshape(spectrum_shape)


def advect(padded, sea_field, courant_x, courant_y):
    flux_y = (
        jnp.maximum(courant_y, 0.0) * padded[..., :-1, :]
        + jnp.minimum(courant_y, 0.0) * padded[..., 1:, :]
    )
    center = padded[..., 1:-1, :]
    widths = [(0, 0)] * (center.ndim - 1) + [(1, 1)]
    padded_x = jnp.pad(center, widths)
    flux_x = (
        jnp.maximum(courant_x, 0.0) * padded_x[..., :-1]
        + jnp.minimum(courant_x, 0.0) * padded_x[..., 1:]
    )
    return (
        center - (flux_x[..., 1:] - flux_x[..., :-1]) - (flux_y[..., 1:, :] - flux_y[..., :-1, :])
    ) * sea_field


def per_device(
    energy,
    heading,
    growth,
    courant,
    dissip,
    mixing,
    transfer,
    pattern,
    regime_winds,
    regime,
    seeds,
    sea_mask,
):
    wind_u, wind_v = strip_winds(regime_winds, regime, seeds)
    widened = energy.astype(jnp.float32)
    drive = (
        wind_u[None] * jnp.cos(heading)[:, None, None]
        + wind_v[None] * jnp.sin(heading)[:, None, None]
    )
    input_term = growth[:, None, None] * jnp.maximum(0.0, drive) * widened
    returned = lax.all_to_all(
        cell_terms(
            lax.all_to_all(energy, "comp", split_axis=1, concat_axis=0, tiled=True),
            mixing,
            transfer,
            pattern,
            dissip,
        ),
        "comp",
        split_axis=0,
        concat_axis=1,
        tiled=True,
    )
    energy_field = widened + input_term + returned.astype(jnp.float32)
    sea_field = sea_mask.astype(jnp.float32)
    courant_x = courant[:, 0][:, None, None]
    courant_y = courant[:, 1][:, None, None]
    for substep in range(SUBSTEPS):
        padded = with_halo(energy_field, (("strip", 1),), 1)
        energy_field = advect(padded, sea_field, courant_x, courant_y)
    return energy_field

def exchange(value, axis, distance):
    count = lax.axis_size(axis)
    return lax.ppermute(value, axis, [(i, i ^ distance) for i in range(count)])


def in_hbm(value):
    return pltpu.with_memory_space_constraint(value, pltpu.MemorySpace.HBM)


def spread_kernel(chips, halo, outer, where, energy_ref, *refs):
    outs, wide = refs[:-1], refs[-1]
    group, rows, width = energy_ref.shape
    for block in range(width // LANES):
        lanes = slice(block * LANES, (block + 1) * LANES)
        wide[block] = (
            energy_ref[:, :, lanes].astype(jnp.float32).reshape(group * rows, LANES)
        )

    def place(out_ref, slot, row):
        for block in range(width // LANES):
            start = slot * width + block * LANES
            picked = wide[block, pl.ds(row, group, stride=rows), :]
            out_ref[:, start : start + LANES] = picked.astype(jnp.bfloat16)

    for m in range(chips):
        chip = jnp.bitwise_xor(where[0], m)
        for slot in range(2):
            first = slot * (rows - halo) if outer else (slot + 1) * halo
            place(outs[m], slot, chip + first)
        if not outer:
            for side in range(2):
                place(outs[chips + side], m, chip + (rows - halo) * where[2 + side])


def spread(where, energy, chips, halo, outer):
    local, rows, width = energy.shape
    block = 3 * GROUP
    sizes = [2 * width] * chips + ([] if outer else [halo * width] * 2)
    return pl.pallas_call(
        functools.partial(spread_kernel, chips, halo, outer),
        grid_spec=pltpu.PrefetchScalarGridSpec(
            num_scalar_prefetch=1,
            grid=(local // block,),
            in_specs=[pl.BlockSpec((block, rows, width), lambda i, w: (i, 0, 0))],
            out_specs=[pl.BlockSpec((block, size), lambda i, w: (i, 0)) for size in sizes],
            scratch_shapes=[pltpu.VMEM((width // LANES, block * rows, LANES), jnp.float32)],
        ),
        out_shape=[pltpu.MemorySpace.HBM((local, size), jnp.bfloat16) for size in sizes],
        compiler_params=pltpu.CompilerParams(vmem_limit_bytes=12 * MIB),
        cost_estimate=pl.CostEstimate(
            flops=energy.size, bytes_accessed=3 * energy.size, transcendentals=0
        ),
        name="spread_outer" if outer else "spread_rest",
    )(where, energy)


def gather_kernel(chips, parts, where, extra_ref, *refs):
    pieces, outs, sems = refs[:chips], refs[chips:-1], refs[-1]
    width = pieces[0].shape[1] // 2
    copies = []
    for side in range(2):
        start = pl.multiple_of(width * where[2 + side], LANES)
        begin = 0
        for index, part in enumerate(parts):
            out = outs[2 * index + side]
            for m in range(chips):
                copies.append(
                    pltpu.make_async_copy(
                        pieces[m].at[begin : begin + part, pl.ds(start, width)],
                        out.at[:part, m * width : (m + 1) * width],
                        sems.at[len(copies)],
                    )
                )
            if index == 0:
                out[part:, :] = extra_ref[side]
            begin += part
    for copy in copies:
        copy.start()
    for copy in copies:
        copy.wait()


def gather_edges(where, extra, landed, parts):
    chips = len(landed)
    width = landed[0].shape[1] // 2
    shapes = [part + (GROUP if index == 0 else 0) for index, part in enumerate(parts)]
    whole = pl.BlockSpec(memory_space=pltpu.VMEM)
    return pl.pallas_call(
        functools.partial(gather_kernel, chips, parts),
        in_specs=[pl.BlockSpec(memory_space=pltpu.SMEM), whole]
        + [pl.BlockSpec(memory_space=pl.ANY)] * chips,
        out_specs=[whole] * (2 * len(parts)),
        out_shape=[
            jax.ShapeDtypeStruct((shape, chips * width), jnp.bfloat16)
            for shape in shapes
            for side in range(2)
        ],
        scratch_shapes=[pltpu.SemaphoreType.DMA((2 * chips * len(parts),))],
        compiler_params=pltpu.CompilerParams(vmem_limit_bytes=4 * MIB),
        cost_estimate=pl.CostEstimate(
            flops=0, bytes_accessed=4 * chips * sum(shapes) * width, transcendentals=0
        ),
        name="gather_edges",
    )(where, extra, *landed)


def weights_kernel(
    chips,
    where,
    row_ref,
    mixing_hbm,
    transfer_hbm,
    first_hbm,
    second_hbm,
    pick_t,
    mixing_ref,
    transfer_ref,
    first_ref,
    second_ref,
    in_sems,
    out_sems,
):
    total = mixing_ref.shape[0]
    local = total // (2 * chips)
    stripe = total // chips
    loads = []
    for m in range(chips):
        block = 2 * jnp.bitwise_xor(where[0], m) + where[1]
        loads.append(
            pltpu.make_async_copy(
                transfer_hbm.at[pl.ds(pl.multiple_of(block * local, GROUP), local), :],
                transfer_ref.at[m * local : (m + 1) * local, :],
                in_sems.at[m],
            )
        )
    loads.append(pltpu.make_async_copy(mixing_hbm, mixing_ref, in_sems.at[chips]))
    for load in loads:
        load.start()
    pick_t[...] = (
        row_ref[...] == lax.broadcasted_iota(jnp.int32, (total, total), 0)
    ).astype(jnp.bfloat16)
    extra = first_ref.shape[0] - total
    first_ref[total:, :] = jnp.ones((extra, total), jnp.bfloat16)
    stores = []

    def send(source, target, start, size):
        store = pltpu.make_async_copy(
            source.at[start : start + size, :],
            target.at[start : start + size, :],
            out_sems.at[len(stores)],
        )
        store.start()
        stores.append(store)

    for load in loads[:chips]:
        load.wait()
    second_ref[...] = lax.dot_general(
        transfer_ref[...],
        pick_t[...],
        (((1,), (1,)), ((), ())),
        preferred_element_type=jnp.float32,
    ).astype(jnp.bfloat16)
    send(second_ref, second_hbm, 0, total // 2)
    loads[chips].wait()
    for start in range(0, total, stripe):
        first_ref[start : start + stripe, :] = jnp.dot(
            pick_t[start : start + stripe, :],
            mixing_ref[...],
            preferred_element_type=jnp.float32,
        ).astype(jnp.bfloat16)
        send(first_ref, first_hbm, start, stripe + (extra if start + stripe == total else 0))
    for store in stores:
        store.wait()


def weights(where, pattern, mixing, transfer, chips):
    total = mixing.shape[0]
    whole = pl.BlockSpec(memory_space=pltpu.VMEM)
    outside = pl.BlockSpec(memory_space=pltpu.MemorySpace.HBM)
    shapes = [(total + GROUP, total), (total // 2, total)]
    return pl.pallas_call(
        functools.partial(weights_kernel, chips),
        in_specs=[pl.BlockSpec(memory_space=pltpu.SMEM)] + [whole] + [outside] * 2,
        out_specs=[outside] * 2,
        out_shape=[pltpu.MemorySpace.HBM(shape, jnp.bfloat16) for shape in shapes],
        scratch_shapes=[pltpu.VMEM((total, total), jnp.bfloat16)] * 2
        + [pltpu.VMEM((total // 2, total), jnp.bfloat16)]
        + [pltpu.VMEM(shape, jnp.bfloat16) for shape in shapes]
        + [pltpu.SemaphoreType.DMA((chips + 1,)), pltpu.SemaphoreType.DMA((chips + 1,))],
        compiler_params=pltpu.CompilerParams(vmem_limit_bytes=20 * MIB),
        cost_estimate=pl.CostEstimate(
            flops=3 * total**3, bytes_accessed=8 * total**2, transcendentals=0
        ),
        name="weights",
    )(where, pattern[None, :], in_hbm(mixing), in_hbm(transfer))


def terms_kernel(chips, where, dissip_ref, first_hbm, second_hbm, *refs):
    pieces, outs = refs[: 2 * chips], refs[2 * chips : 3 * chips]
    spectra, product, result, first_ref, second_ref, in_sems, weight_sems, out_sems = refs[
        3 * chips :
    ]
    total = spectra.shape[0]
    local = total // (2 * chips)
    stripe = total // chips
    extra = first_ref.shape[0] - total

    def start_of(m, other):
        core = jnp.bitwise_xor(where[1], other)
        block = 2 * jnp.bitwise_xor(where[0], m) + core
        return pl.multiple_of(block * local, GROUP)

    copies = [
        pltpu.make_async_copy(
            pieces[m + other * chips],
            spectra.at[pl.ds(start_of(m, other), local), :],
            in_sems.at[2 * m + other],
        )
        for m in range(chips)
        for other in range(2)
    ]
    stripes = []
    for index in range(chips):
        begin = index * stripe
        end = begin + stripe + (extra if index == chips - 1 else 0)
        stripes.append(
            pltpu.make_async_copy(
                first_hbm.at[begin:end, :], first_ref.at[begin:end, :], weight_sems.at[index]
            )
        )
    load = pltpu.make_async_copy(second_hbm, second_ref, weight_sems.at[chips])
    for copy in [*copies, *stripes, load]:
        copy.start()
    for copy in copies:
        copy.wait()

    for index in range(chips):
        start = index * stripe
        last = index == chips - 1
        stripes[index].wait()
        mixed = jnp.dot(
            first_ref[start : start + stripe + (extra if last else 0), :],
            spectra[...],
            preferred_element_type=jnp.float32,
        )
        product[start : start + stripe, :] = (
            mixed[:stripe] * spectra[start : start + stripe, :].astype(jnp.float32)
        ).astype(jnp.bfloat16)
        if last:
            mean = mixed[stripe : stripe + 1] * (1.0 / total)
    load.wait()
    sent = []
    for m in range(chips):
        rows = pl.ds(start_of(m, 0), local)
        mine = slice(m * local, (m + 1) * local)
        nonlinear = jnp.dot(
            second_ref[mine, :], product[...], preferred_element_type=jnp.float32
        )
        own = spectra[rows, :].astype(jnp.float32)
        result[mine, :] = (nonlinear - dissip_ref[rows, :] * mean * own).astype(jnp.bfloat16)
        copy = pltpu.make_async_copy(result.at[mine, :], outs[m], out_sems.at[m])
        copy.start()
        sent.append(copy)
    for copy in sent:
        copy.wait()


def source_terms(where, first, second, dissip, near, far):
    chips = len(near)
    local, cells = near[0].shape
    total = 2 * chips * local
    outside = pl.BlockSpec(memory_space=pltpu.MemorySpace.HBM)
    return pl.pallas_call(
        functools.partial(terms_kernel, chips),
        in_specs=[
            pl.BlockSpec(memory_space=pltpu.SMEM),
            pl.BlockSpec(memory_space=pltpu.VMEM),
            outside,
            outside,
        ]
        + [pl.BlockSpec(memory_space=pl.ANY)] * (2 * chips),
        out_specs=[outside] * chips,
        out_shape=[pltpu.MemorySpace.HBM((local, cells), jnp.bfloat16)] * chips,
        scratch_shapes=[
            pltpu.VMEM((total, cells), jnp.bfloat16),
            pltpu.VMEM((total, cells), jnp.bfloat16),
            pltpu.VMEM((total // 2, cells), jnp.bfloat16),
            pltpu.VMEM(first.shape, jnp.bfloat16),
            pltpu.VMEM(second.shape, jnp.bfloat16),
            pltpu.SemaphoreType.DMA((2 * chips,)),
            pltpu.SemaphoreType.DMA((chips + 1,)),
            pltpu.SemaphoreType.DMA((chips,)),
        ],
        compiler_params=pltpu.CompilerParams(vmem_limit_bytes=18 * MIB),
        cost_estimate=pl.CostEstimate(
            flops=3 * total * total * cells, bytes_accessed=8 * total * cells, transcendentals=0
        ),
        name="source_terms",
    )(where, dissip[:, None], in_hbm(first), in_hbm(second), *map(in_hbm, [*near, *far]))


def propagate_kernel(chips, halo, where, coef_ref, fields_ref, *refs):
    count = 2 * chips + 2
    energies, edges, terms = refs[:count], refs[count : count + 2], refs[count + 2 : 2 * count + 2]
    out_ref, field, turned, weather = refs[-4:]
    rows, blocks, group, lanes = field.shape
    width = blocks * lanes
    inner = rows - 2 * halo

    def column(at, number, index):
        return jnp.broadcast_to(coef_ref[at : at + number, index : index + 1], (number, lanes))

    cosine, sine = column(0, group, 0), column(0, group, 1)

    firsts = [(halo + inner) * where[2 + side] for side in range(2)]

    @pl.when(pl.program_id(0) == 0)
    def _():
        for index in range(3):
            for row in range(inner):
                for b in range(blocks):
                    part = slice(b * lanes, (b + 1) * lanes)
                    weather[index, halo + row, b] = jnp.broadcast_to(
                        fields_ref[index, row : row + 1, part], (SUBLANES, lanes)
                    )
        for side in range(2):
            pieces = edges[side][...].astype(jnp.float32)
            for index in range(3):
                value = pieces[3 * index : 3 * index + 1]
                value = value + pieces[3 * index + 1 : 3 * index + 2]
                value = value + pieces[3 * index + 2 : 3 * index + 3]
                value = jnp.where(where[4 + side] == 1, value, 0.0)
                for row in range(halo):
                    for b in range(blocks):
                        at = row * width + b * lanes
                        weather[index, firsts[side] + row, b] = jnp.broadcast_to(
                            value[:, at : at + lanes], (SUBLANES, lanes)
                        )

    def force(energy_ref, term_ref, slot, row, valid=None):
        for b in range(blocks):
            at = slice(slot * width + b * lanes, slot * width + (b + 1) * lanes)
            wind_u = jnp.concatenate([weather[0, row, b]] * (group // SUBLANES))
            wind_v = jnp.concatenate([weather[1, row, b]] * (group // SUBLANES))
            drive = wind_u * cosine + wind_v * sine
            value = energy_ref[:, at].astype(jnp.float32) * (
                1.0 + jnp.maximum(drive, 0.0)
            ) + term_ref[:, at].astype(jnp.float32)
            if valid is not None:
                value = jnp.where(valid == 1, value, 0.0)
            field[row, b] = value

    for m in range(chips):
        chip = jnp.bitwise_xor(where[0], m)
        for slot in range(2):
            force(energies[m], terms[m], slot, halo + chip + slot * (inner - halo))
            force(energies[chips + m], terms[chips + m], slot, halo + chip + (slot + 1) * halo)
        for side in range(2):
            index = 2 * chips + side
            force(energies[index], terms[index], m, firsts[side] + chip, where[4 + side])

    lane = lax.broadcasted_iota(jnp.int32, (SUBLANES, lanes), 1)
    for at in range(0, group, SUBLANES):
        here = slice(at, at + SUBLANES)
        keep, west, east, south, north = [column(at, SUBLANES, i) for i in range(2, 7)]
        from_west, from_south = west > 0.0, south > 0.0
        source = jnp.bitwise_and(jnp.where(from_west, lane - 1, lane + 1), lanes - 1)
        first_lane = jnp.logical_and(from_west, lane == 0)
        last_lane = jnp.logical_and(jnp.logical_not(from_west), lane == lanes - 1)
        along, across = west + east, south + north
        for substep in range(1, halo + 1):
            before = [field[substep - 1, b, here] for b in range(blocks)]
            center = [field[substep, b, here] for b in range(blocks)]
            for row in range(substep, rows - substep):
                after = [field[row + 1, b, here] for b in range(blocks)]
                moved = [jnp.take_along_axis(value, source, axis=1) for value in center]
                for b in range(blocks):
                    beside = jnp.where(first_lane, moved[b - 1] if b > 0 else 0.0, moved[b])
                    beside = jnp.where(
                        last_lane, moved[b + 1] if b < blocks - 1 else 0.0, beside
                    )
                    upwind = jnp.where(from_south, before[b], after[b])
                    value = (center[b] * keep + beside * along + upwind * across) * weather[
                        2, row, b
                    ]
                    if substep < halo:
                        field[row, b, here] = value
                    else:
                        turned[
                            b, pl.ds(at * inner + row - halo, SUBLANES, stride=inner), :
                        ] = value
                before, center = center, after
    for b in range(blocks):
        out_ref[:, b * lanes : (b + 1) * lanes] = turned[b]


def propagate(where, coef, fields, energies, edges, terms, begin, part, previous, halo):
    chips = (len(energies) - 2) // 2
    local = energies[0].shape[0]
    inner, width = fields.shape[1:]
    rows = inner + 2 * halo
    steps = part // GROUP
    base = begin // GROUP
    last = edges[0].shape[0] // GROUP - 1
    cells, edge = energies[0].shape[1], energies[-1].shape[1]
    shape = jax.ShapeDtypeStruct((local * inner, width), jnp.float32)
    at_base = lambda i, w: (base + i, 0)
    in_specs = (
        [
            pl.BlockSpec((GROUP, coef.shape[1]), at_base),
            pl.BlockSpec(fields.shape, lambda i, w: (0, 0, 0)),
        ]
        + [pl.BlockSpec((GROUP, cells), at_base)] * (2 * chips)
        + [pl.BlockSpec((GROUP, edge), at_base)] * 2
        + [pl.BlockSpec((GROUP, edge), lambda i, w: (last, 0))] * 2
        + [pl.BlockSpec((GROUP, cells), at_base)] * (2 * chips)
        + [pl.BlockSpec((GROUP, edge), lambda i, w: (i, 0))] * 2
    )
    operands = [where, coef, fields, *map(in_hbm, energies), *edges]
    operands += [*map(in_hbm, terms[: 2 * chips]), *terms[2 * chips :]]
    aliases = {}
    kernel = functools.partial(propagate_kernel, chips, halo)
    if previous is not None:
        aliases = {len(operands): 0}
        operands.append(previous)
        in_specs.append(pl.BlockSpec(memory_space=pl.ANY))
    return pl.pallas_call(
        kernel,
        grid_spec=pltpu.PrefetchScalarGridSpec(
            num_scalar_prefetch=1,
            grid=(steps,),
            in_specs=in_specs,
            out_specs=pl.BlockSpec((GROUP * inner, width), lambda i, w: (base + i, 0)),
            scratch_shapes=[
                pltpu.VMEM((rows, width // LANES, GROUP, LANES), jnp.float32),
                pltpu.VMEM((width // LANES, GROUP * inner, LANES), jnp.float32),
                pltpu.VMEM((3, rows, width // LANES, SUBLANES, LANES), jnp.float32),
            ],
        ),
        out_shape=shape,
        input_output_aliases=aliases,
        compiler_params=pltpu.CompilerParams(vmem_limit_bytes=10 * MIB),
        cost_estimate=pl.CostEstimate(
            flops=60 * shape.size * part // local,
            bytes_accessed=8 * shape.size * part // local,
            transcendentals=0,
        ),
        name="propagate",
    )(*operands)


def thirds(value):
    pieces, rest = [], value
    for _ in range(3):
        piece = lax.reduce_precision(rest, 8, 7)
        pieces.append(piece)
        rest = rest - piece
    stacked = jnp.stack(pieces, axis=1).reshape(3 * value.shape[0], value.shape[1])
    return jnp.pad(stacked, ((0, GROUP - stacked.shape[0]), (0, 0))).astype(jnp.bfloat16)


def pair_up(value, start):
    count = lax.axis_size("strip")
    target = list(range(count))
    for i in range(start, count - 1, 2):
        target[i], target[i + 1] = i + 1, i
    return lax.ppermute(value, "strip", list(enumerate(target)))


def per_device_paired(
    energy,
    heading,
    growth,
    courant,
    dissip,
    mixing,
    transfer,
    pattern,
    regime_winds,
    regime,
    seeds,
    sea_mask,
):
    chips = lax.axis_size("comp") // 2
    local, rows, width = energy.shape
    halo = SUBSTEPS
    units = local // GROUP
    parts = (units // 2 * GROUP, (units - units // 2) * GROUP)
    me, strip, strips = lax.axis_index("comp"), lax.axis_index("strip"), lax.axis_size("strip")
    chip, odd = me // 2, strip % 2
    has_above = (strip > 0).astype(jnp.int32)
    has_below = (strip < strips - 1).astype(jnp.int32)
    where = jnp.stack(
        [
            chip,
            me % 2,
            1 - odd,
            odd,
            jnp.where(odd == 1, has_above, has_below),
            jnp.where(odd == 1, has_below, has_above),
        ]
    ).astype(jnp.int32)

    outer = spread(where, energy, chips, halo, True)
    rest = spread(where, energy, chips, halo, False)
    near_outer = [outer[0]] + [exchange(outer[m], "comp", 2 * m) for m in range(1, chips)]
    first, second = weights(where, pattern, mixing, transfer, chips)
    near_outer, rest, first, second = lax.optimization_barrier(
        (near_outer, rest, first, second)
    )
    middle, sides = rest[:chips], rest[chips:]
    near_middle = [middle[0]] + [exchange(middle[m], "comp", 2 * m) for m in range(1, chips)]
    energies = [*outer, *middle] + [pair_up(sides[side], side) for side in range(2)]

    far_outer = [exchange(value, "comp", 1) for value in near_outer]
    sent_outer = source_terms(where, first, second, dissip, near_outer, far_outer)
    landed_outer = [sent_outer[0]] + [
        exchange(sent_outer[m], "comp", 2 * m) for m in range(1, chips)
    ]

    regime_winds, regime, seeds, sea_mask, _ = lax.optimization_barrier(
        (regime_winds, regime, seeds, sea_mask, sent_outer)
    )
    wind_u, wind_v = strip_winds(regime_winds, regime, seeds)
    fields = jnp.stack([wind_u, wind_v, sea_mask.astype(jnp.float32)])
    upper, lower = fields[:, :halo], fields[:, rows - halo :]
    extra = jnp.stack(
        [
            thirds(jnp.where(odd == 1, upper, lower).reshape(3, -1)),
            thirds(jnp.where(odd == 1, lower, upper).reshape(3, -1)),
        ]
    )
    along, across = courant[:, 0], courant[:, 1]
    coef = jnp.stack(
        [
            growth * jnp.cos(heading),
            growth * jnp.sin(heading),
            1.0 - jnp.abs(along) - jnp.abs(across),
            jnp.maximum(along, 0.0),
            -jnp.minimum(along, 0.0),
            jnp.maximum(across, 0.0),
            -jnp.minimum(across, 0.0),
            jnp.zeros_like(along),
        ],
        axis=1,
    )

    near_middle, sent_outer = lax.optimization_barrier((near_middle, sent_outer))
    far_middle = [exchange(value, "comp", 1) for value in near_middle]
    sent_middle = source_terms(where, first, second, dissip, near_middle, far_middle)
    landed_middle = [sent_middle[0]] + [
        exchange(sent_middle[m], "comp", 2 * m) for m in range(1, chips)
    ]

    edges = gather_edges(where, extra, landed_outer, parts)
    edges = [pair_up(edge, index % 2) for index, edge in enumerate(edges)]
    landed = [*landed_outer, *landed_middle]
    result = None
    for j in range(len(parts)):
        result = propagate(
            where,
            coef,
            fields,
            energies,
            edges[:2],
            landed + edges[2 * j : 2 * j + 2],
            sum(parts[:j]),
            parts[j],
            result,
            halo,
        )
    return result.reshape(local, rows, width)


def solution(mesh):
    placed = (
        P("comp", "strip", None),
        P("comp"),
        P("comp"),
        P("comp", None),
        P(),
        P(),
        P(),
        P(),
        P(),
        P("strip", None),
        P("strip", None),
        P("strip", None),
    )
    paired = mesh.shape["comp"] == 2 * SUBSTEPS
    body = per_device_paired if paired else per_device
    return jax.shard_map(
        body, mesh=mesh, in_specs=placed, out_specs=P("comp", "strip", None), check_vma=False
    )
```

```python
import functools
import jax
import jax.numpy as jnp
from jax import lax
from jax.experimental import pallas as pl
from jax.experimental.pallas import tpu as pltpu
from jax.sharding import PartitionSpec as P

SUBSTEPS = 4
TILE_ROWS = 2
TILE_COLS = 16
GROUP = 16
SUBLANES = 8
LANES = 128
MIB = 1 << 20


def with_halo(block, sides, width):
    for axis, dim in sides:
        count = lax.axis_size(axis)
        forward = [(i, i + 1) for i in range(count - 1)]
        backward = [(target, source) for source, target in forward]
        low = lax.ppermute(
            lax.slice_in_dim(block, block.shape[dim] - width, None, axis=dim), axis, forward
        )
        high = lax.ppermute(lax.slice_in_dim(block, 0, width, axis=dim), axis, backward)
        block = jnp.concatenate([low, block, high], axis=dim)
    return block


def strip_winds(regime_winds, regime, seeds):
    levels = jnp.arange(regime_winds.shape[0], dtype=jnp.int32)
    onehot = (regime[..., None] == levels).astype(jnp.float32)
    base_u = jnp.sum(onehot * regime_winds[:, 0], axis=-1)
    base_v = jnp.sum(onehot * regime_winds[:, 1], axis=-1)
    tile_u = base_u + 0.25 * (seeds % 13 - 6).astype(jnp.float32)
    tile_v = base_v + 0.4 * (seeds % 7 - 3).astype(jnp.float32)
    wind_u = jnp.repeat(jnp.repeat(tile_u, TILE_ROWS, axis=0), TILE_COLS, axis=1)
    wind_v = jnp.repeat(jnp.repeat(tile_v, TILE_ROWS, axis=0), TILE_COLS, axis=1)
    return (wind_u, wind_v)


def cell_terms(spectra, mixing, transfer, pattern, dissip):
    spectrum_shape = spectra.shape
    flattened = spectra.reshape(spectrum_shape[0], -1)
    mixed_terms = jnp.dot(mixing, flattened, preferred_element_type=jnp.float32)
    partner = jnp.take(flattened, pattern, axis=0)
    product = (mixed_terms * partner.astype(jnp.float32)).astype(jnp.bfloat16)
    nonlinear = jnp.dot(transfer, product, preferred_element_type=jnp.float32)
    widened = flattened.astype(jnp.float32)
    mean_energy = jnp.sum(widened, axis=0) / spectrum_shape[0]
    result = nonlinear - dissip[:, None] * mean_energy[None, :] * widened
    return result.astype(jnp.bfloat16).reshape(spectrum_shape)


def advect(padded, sea_field, courant_x, courant_y):
    flux_y = (
        jnp.maximum(courant_y, 0.0) * padded[..., :-1, :]
        + jnp.minimum(courant_y, 0.0) * padded[..., 1:, :]
    )
    center = padded[..., 1:-1, :]
    widths = [(0, 0)] * (center.ndim - 1) + [(1, 1)]
    padded_x = jnp.pad(center, widths)
    flux_x = (
        jnp.maximum(courant_x, 0.0) * padded_x[..., :-1]
        + jnp.minimum(courant_x, 0.0) * padded_x[..., 1:]
    )
    return (
        center - (flux_x[..., 1:] - flux_x[..., :-1]) - (flux_y[..., 1:, :] - flux_y[..., :-1, :])
    ) * sea_field


def per_device(
    energy,
    heading,
    growth,
    courant,
    dissip,
    mixing,
    transfer,
    pattern,
    regime_winds,
    regime,
    seeds,
    sea_mask,
):
    wind_u, wind_v = strip_winds(regime_winds, regime, seeds)
    widened = energy.astype(jnp.float32)
    drive = (
        wind_u[None] * jnp.cos(heading)[:, None, None]
        + wind_v[None] * jnp.sin(heading)[:, None, None]
    )
    input_term = growth[:, None, None] * jnp.maximum(0.0, drive) * widened
    returned = lax.all_to_all(
        cell_terms(
            lax.all_to_all(energy, "comp", split_axis=1, concat_axis=0, tiled=True),
            mixing,
            transfer,
            pattern,
            dissip,
        ),
        "comp",
        split_axis=0,
        concat_axis=1,
        tiled=True,
    )
    energy_field = widened + input_term + returned.astype(jnp.float32)
    sea_field = sea_mask.astype(jnp.float32)
    courant_x = courant[:, 0][:, None, None]
    courant_y = courant[:, 1][:, None, None]
    for substep in range(SUBSTEPS):
        padded = with_halo(energy_field, (("strip", 1),), 1)
        energy_field = advect(padded, sea_field, courant_x, courant_y)
    return energy_field

def exchange(value, axis, distance):
    count = lax.axis_size(axis)
    return lax.ppermute(value, axis, [(i, i ^ distance) for i in range(count)])


def in_hbm(value):
    return pltpu.with_memory_space_constraint(value, pltpu.MemorySpace.HBM)


def spread_kernel(chips, halo, outer, where, energy_ref, *refs):
    count = chips + (0 if outer else 2)
    targets, outs, (wide, sems) = refs[:count], refs[count : 2 * count], refs[2 * count :]
    local, rows, width = energy_ref.shape
    group = wide.shape[1] // rows
    sent = []
    for index in range(local // group):
        mine = slice(index * group, (index + 1) * group)
        for block in range(width // LANES):
            lanes = slice(block * LANES, (block + 1) * LANES)
            wide[block] = (
                energy_ref[mine, :, lanes].astype(jnp.float32).reshape(group * rows, LANES)
            )

        def place(out_ref, slot, row):
            for block in range(width // LANES):
                start = slot * width + block * LANES
                picked = wide[block, pl.ds(row, group, stride=rows), :]
                out_ref[mine, start : start + LANES] = picked.astype(jnp.bfloat16)

        for m in range(chips):
            chip = jnp.bitwise_xor(where[0], m)
            for slot in range(2):
                first = slot * (rows - halo) if outer else (slot + 1) * halo
                place(outs[m], slot, chip + first)
            if not outer:
                for side in range(2):
                    place(outs[chips + side], m, chip + (rows - halo) * where[2 + side])
        for number in range(count):
            copy = pltpu.make_async_copy(
                outs[number].at[mine, :], targets[number].at[mine, :], sems.at[index, number]
            )
            copy.start()
            sent.append(copy)
    for copy in sent:
        copy.wait()


def spread(where, energy, chips, halo, outer):
    local, rows, width = energy.shape
    block = 3 * GROUP
    sizes = [2 * width] * chips + ([] if outer else [halo * width] * 2)
    return pl.pallas_call(
        functools.partial(spread_kernel, chips, halo, outer),
        in_specs=[
            pl.BlockSpec(memory_space=pltpu.SMEM),
            pl.BlockSpec(memory_space=pltpu.VMEM),
        ],
        out_specs=[pl.BlockSpec(memory_space=pltpu.MemorySpace.HBM)] * len(sizes),
        out_shape=[pltpu.MemorySpace.HBM((local, size), jnp.bfloat16) for size in sizes],
        scratch_shapes=[pltpu.VMEM((local, size), jnp.bfloat16) for size in sizes]
        + [
            pltpu.VMEM((width // LANES, block * rows, LANES), jnp.float32),
            pltpu.SemaphoreType.DMA((local // block, len(sizes))),
        ],
        compiler_params=pltpu.CompilerParams(vmem_limit_bytes=12 * MIB),
        cost_estimate=pl.CostEstimate(
            flops=energy.size, bytes_accessed=3 * energy.size, transcendentals=0
        ),
        name="spread_outer" if outer else "spread_rest",
    )(where, energy)


def gather_kernel(chips, parts, where, extra_ref, *refs):
    pieces, outs, sems = refs[:chips], refs[chips:-1], refs[-1]
    width = pieces[0].shape[1] // 2
    copies = []
    for side in range(2):
        start = pl.multiple_of(width * where[2 + side], LANES)
        begin = 0
        for index, part in enumerate(parts):
            out = outs[2 * index + side]
            for m in range(chips):
                copies.append(
                    pltpu.make_async_copy(
                        pieces[m].at[begin : begin + part, pl.ds(start, width)],
                        out.at[:part, m * width : (m + 1) * width],
                        sems.at[len(copies)],
                    )
                )
            if index == 0:
                out[part:, :] = extra_ref[side]
            begin += part
    for copy in copies:
        copy.start()
    for copy in copies:
        copy.wait()


def gather_edges(where, extra, landed, parts):
    chips = len(landed)
    width = landed[0].shape[1] // 2
    shapes = [part + (GROUP if index == 0 else 0) for index, part in enumerate(parts)]
    whole = pl.BlockSpec(memory_space=pltpu.VMEM)
    return pl.pallas_call(
        functools.partial(gather_kernel, chips, parts),
        in_specs=[pl.BlockSpec(memory_space=pltpu.SMEM), whole]
        + [pl.BlockSpec(memory_space=pl.ANY)] * chips,
        out_specs=[whole] * (2 * len(parts)),
        out_shape=[
            jax.ShapeDtypeStruct((shape, chips * width), jnp.bfloat16)
            for shape in shapes
            for side in range(2)
        ],
        scratch_shapes=[pltpu.SemaphoreType.DMA((2 * chips * len(parts),))],
        compiler_params=pltpu.CompilerParams(vmem_limit_bytes=4 * MIB),
        cost_estimate=pl.CostEstimate(
            flops=0, bytes_accessed=4 * chips * sum(shapes) * width, transcendentals=0
        ),
        name="gather_edges",
    )(where, extra, *landed)


def weights_kernel(
    chips,
    where,
    row_ref,
    mixing_hbm,
    transfer_hbm,
    first_hbm,
    second_hbm,
    pick_t,
    mixing_ref,
    transfer_ref,
    first_ref,
    second_ref,
    in_sems,
    out_sems,
):
    total = mixing_ref.shape[0]
    local = total // (2 * chips)
    stripe = total // chips
    loads = []
    for m in range(chips):
        block = 2 * jnp.bitwise_xor(where[0], m) + where[1]
        loads.append(
            pltpu.make_async_copy(
                transfer_hbm.at[pl.ds(pl.multiple_of(block * local, GROUP), local), :],
                transfer_ref.at[m * local : (m + 1) * local, :],
                in_sems.at[m],
            )
        )
    loads.append(pltpu.make_async_copy(mixing_hbm, mixing_ref, in_sems.at[chips]))
    for load in loads:
        load.start()
    pick_t[...] = (
        row_ref[...] == lax.broadcasted_iota(jnp.int32, (total, total), 0)
    ).astype(jnp.bfloat16)
    extra = first_ref.shape[0] - total
    first_ref[total:, :] = jnp.ones((extra, total), jnp.bfloat16)
    stores = []

    def send(source, target, start, size):
        store = pltpu.make_async_copy(
            source.at[start : start + size, :],
            target.at[start : start + size, :],
            out_sems.at[len(stores)],
        )
        store.start()
        stores.append(store)

    for load in loads[:chips]:
        load.wait()
    second_ref[...] = lax.dot_general(
        transfer_ref[...],
        pick_t[...],
        (((1,), (1,)), ((), ())),
        preferred_element_type=jnp.float32,
    ).astype(jnp.bfloat16)
    send(second_ref, second_hbm, 0, total // 2)
    loads[chips].wait()
    for start in range(0, total, stripe):
        first_ref[start : start + stripe, :] = jnp.dot(
            pick_t[start : start + stripe, :],
            mixing_ref[...],
            preferred_element_type=jnp.float32,
        ).astype(jnp.bfloat16)
        send(first_ref, first_hbm, start, stripe + (extra if start + stripe == total else 0))
    for store in stores:
        store.wait()


def weights(where, pattern, mixing, transfer, chips):
    total = mixing.shape[0]
    whole = pl.BlockSpec(memory_space=pltpu.VMEM)
    outside = pl.BlockSpec(memory_space=pltpu.MemorySpace.HBM)
    shapes = [(total + GROUP, total), (total // 2, total)]
    return pl.pallas_call(
        functools.partial(weights_kernel, chips),
        in_specs=[pl.BlockSpec(memory_space=pltpu.SMEM)] + [whole] + [outside] * 2,
        out_specs=[outside] * 2,
        out_shape=[pltpu.MemorySpace.HBM(shape, jnp.bfloat16) for shape in shapes],
        scratch_shapes=[pltpu.VMEM((total, total), jnp.bfloat16)] * 2
        + [pltpu.VMEM((total // 2, total), jnp.bfloat16)]
        + [pltpu.VMEM(shape, jnp.bfloat16) for shape in shapes]
        + [pltpu.SemaphoreType.DMA((chips + 1,)), pltpu.SemaphoreType.DMA((chips + 1,))],
        compiler_params=pltpu.CompilerParams(vmem_limit_bytes=20 * MIB),
        cost_estimate=pl.CostEstimate(
            flops=3 * total**3, bytes_accessed=8 * total**2, transcendentals=0
        ),
        name="weights",
    )(where, pattern[None, :], in_hbm(mixing), in_hbm(transfer))


def terms_kernel(chips, where, dissip_ref, first_hbm, second_hbm, *refs):
    pieces, outs = refs[: 2 * chips], refs[2 * chips : 3 * chips]
    spectra, product, result, first_ref, second_ref, in_sems, weight_sems, out_sems = refs[
        3 * chips :
    ]
    total = spectra.shape[0]
    local = total // (2 * chips)
    stripe = total // chips
    extra = first_ref.shape[0] - total

    def start_of(m, other):
        core = jnp.bitwise_xor(where[1], other)
        block = 2 * jnp.bitwise_xor(where[0], m) + core
        return pl.multiple_of(block * local, GROUP)

    copies = [
        pltpu.make_async_copy(
            pieces[m + other * chips],
            spectra.at[pl.ds(start_of(m, other), local), :],
            in_sems.at[2 * m + other],
        )
        for m in range(chips)
        for other in range(2)
    ]
    stripes = []
    for index in range(chips):
        begin = index * stripe
        end = begin + stripe + (extra if index == chips - 1 else 0)
        stripes.append(
            pltpu.make_async_copy(
                first_hbm.at[begin:end, :], first_ref.at[begin:end, :], weight_sems.at[index]
            )
        )
    load = pltpu.make_async_copy(second_hbm, second_ref, weight_sems.at[chips])
    for copy in [*copies, stripes[0]]:
        copy.start()
    for copy in copies:
        copy.wait()
    for copy in [*stripes[1:], load]:
        copy.start()

    for index in range(chips):
        start = index * stripe
        last = index == chips - 1
        stripes[index].wait()
        mixed = jnp.dot(
            first_ref[start : start + stripe + (extra if last else 0), :],
            spectra[...],
            preferred_element_type=jnp.float32,
        )
        product[start : start + stripe, :] = (
            mixed[:stripe] * spectra[start : start + stripe, :].astype(jnp.float32)
        ).astype(jnp.bfloat16)
        if last:
            mean = mixed[stripe : stripe + 1] * (1.0 / total)
    load.wait()
    sent = []
    for m in range(chips):
        rows = pl.ds(start_of(m, 0), local)
        mine = slice(m * local, (m + 1) * local)
        nonlinear = jnp.dot(
            second_ref[mine, :], product[...], preferred_element_type=jnp.float32
        )
        own = spectra[rows, :].astype(jnp.float32)
        result[mine, :] = (nonlinear - dissip_ref[rows, :] * mean * own).astype(jnp.bfloat16)
        copy = pltpu.make_async_copy(result.at[mine, :], outs[m], out_sems.at[m])
        copy.start()
        sent.append(copy)
    for copy in sent:
        copy.wait()


def source_terms(where, first, second, dissip, near, far):
    chips = len(near)
    local, cells = near[0].shape
    total = 2 * chips * local
    outside = pl.BlockSpec(memory_space=pltpu.MemorySpace.HBM)
    return pl.pallas_call(
        functools.partial(terms_kernel, chips),
        in_specs=[
            pl.BlockSpec(memory_space=pltpu.SMEM),
            pl.BlockSpec(memory_space=pltpu.VMEM),
            outside,
            outside,
        ]
        + [pl.BlockSpec(memory_space=pl.ANY)] * (2 * chips),
        out_specs=[outside] * chips,
        out_shape=[pltpu.MemorySpace.HBM((local, cells), jnp.bfloat16)] * chips,
        scratch_shapes=[
            pltpu.VMEM((total, cells), jnp.bfloat16),
            pltpu.VMEM((total, cells), jnp.bfloat16),
            pltpu.VMEM((total // 2, cells), jnp.bfloat16),
            pltpu.VMEM(first.shape, jnp.bfloat16),
            pltpu.VMEM(second.shape, jnp.bfloat16),
            pltpu.SemaphoreType.DMA((2 * chips,)),
            pltpu.SemaphoreType.DMA((chips + 1,)),
            pltpu.SemaphoreType.DMA((chips,)),
        ],
        compiler_params=pltpu.CompilerParams(vmem_limit_bytes=18 * MIB),
        cost_estimate=pl.CostEstimate(
            flops=3 * total * total * cells, bytes_accessed=8 * total * cells, transcendentals=0
        ),
        name="source_terms",
    )(where, dissip[:, None], in_hbm(first), in_hbm(second), *map(in_hbm, [*near, *far]))


def propagate_kernel(chips, halo, where, coef_ref, fields_ref, *refs):
    count = 2 * chips + 2
    energies, edges, terms = refs[:count], refs[count : count + 2], refs[count + 2 : 2 * count + 2]
    out_ref, field, turned, weather = refs[-4:]
    rows, blocks, group, lanes = field.shape
    width = blocks * lanes
    inner = rows - 2 * halo

    def column(at, number, index):
        return jnp.broadcast_to(coef_ref[at : at + number, index : index + 1], (number, lanes))

    cosine, sine = column(0, group, 0), column(0, group, 1)

    firsts = [(halo + inner) * where[2 + side] for side in range(2)]

    @pl.when(pl.program_id(0) == 0)
    def _():
        for index in range(3):
            for row in range(inner):
                for b in range(blocks):
                    part = slice(b * lanes, (b + 1) * lanes)
                    weather[index, halo + row, b] = jnp.broadcast_to(
                        fields_ref[index, row : row + 1, part], (SUBLANES, lanes)
                    )
        for side in range(2):
            pieces = edges[side][...].astype(jnp.float32)
            for index in range(3):
                value = pieces[3 * index : 3 * index + 1]
                value = value + pieces[3 * index + 1 : 3 * index + 2]
                value = value + pieces[3 * index + 2 : 3 * index + 3]
                value = jnp.where(where[4 + side] == 1, value, 0.0)
                for row in range(halo):
                    for b in range(blocks):
                        at = row * width + b * lanes
                        weather[index, firsts[side] + row, b] = jnp.broadcast_to(
                            value[:, at : at + lanes], (SUBLANES, lanes)
                        )

    def force(energy_ref, term_ref, slot, row, valid=None):
        for b in range(blocks):
            at = slice(slot * width + b * lanes, slot * width + (b + 1) * lanes)
            wind_u = jnp.concatenate([weather[0, row, b]] * (group // SUBLANES))
            wind_v = jnp.concatenate([weather[1, row, b]] * (group // SUBLANES))
            drive = wind_u * cosine + wind_v * sine
            value = energy_ref[:, at].astype(jnp.float32) * (
                1.0 + jnp.maximum(drive, 0.0)
            ) + term_ref[:, at].astype(jnp.float32)
            if valid is not None:
                value = jnp.where(valid == 1, value, 0.0)
            field[row, b] = value

    for m in range(chips):
        chip = jnp.bitwise_xor(where[0], m)
        for slot in range(2):
            force(energies[m], terms[m], slot, halo + chip + slot * (inner - halo))
            force(energies[chips + m], terms[chips + m], slot, halo + chip + (slot + 1) * halo)
        for side in range(2):
            index = 2 * chips + side
            force(energies[index], terms[index], m, firsts[side] + chip, where[4 + side])

    lane = lax.broadcasted_iota(jnp.int32, (SUBLANES, lanes), 1)
    for at in range(0, group, SUBLANES):
        here = slice(at, at + SUBLANES)
        keep, west, east, south, north = [column(at, SUBLANES, i) for i in range(2, 7)]
        from_west, from_south = west > 0.0, south > 0.0
        source = jnp.bitwise_and(jnp.where(from_west, lane - 1, lane + 1), lanes - 1)
        first_lane = jnp.logical_and(from_west, lane == 0)
        last_lane = jnp.logical_and(jnp.logical_not(from_west), lane == lanes - 1)
        along, across = west + east, south + north
        for substep in range(1, halo + 1):
            before = [field[substep - 1, b, here] for b in range(blocks)]
            center = [field[substep, b, here] for b in range(blocks)]
            for row in range(substep, rows - substep):
                after = [field[row + 1, b, here] for b in range(blocks)]
                moved = [jnp.take_along_axis(value, source, axis=1) for value in center]
                for b in range(blocks):
                    beside = jnp.where(first_lane, moved[b - 1] if b > 0 else 0.0, moved[b])
                    beside = jnp.where(
                        last_lane, moved[b + 1] if b < blocks - 1 else 0.0, beside
                    )
                    upwind = jnp.where(from_south, before[b], after[b])
                    value = (center[b] * keep + beside * along + upwind * across) * weather[
                        2, row, b
                    ]
                    if substep < halo:
                        field[row, b, here] = value
                    else:
                        turned[
                            b, pl.ds(at * inner + row - halo, SUBLANES, stride=inner), :
                        ] = value
                before, center = center, after
    for b in range(blocks):
        out_ref[:, b * lanes : (b + 1) * lanes] = turned[b]


def propagate(where, coef, fields, energies, edges, terms, begin, part, previous, halo):
    chips = (len(energies) - 2) // 2
    local = energies[0].shape[0]
    inner, width = fields.shape[1:]
    rows = inner + 2 * halo
    steps = part // GROUP
    base = begin // GROUP
    last = edges[0].shape[0] // GROUP - 1
    cells, edge = energies[0].shape[1], energies[-1].shape[1]
    shape = jax.ShapeDtypeStruct((local * inner, width), jnp.float32)
    at_base = lambda i, w: (base + i, 0)
    in_specs = (
        [
            pl.BlockSpec((GROUP, coef.shape[1]), at_base),
            pl.BlockSpec(fields.shape, lambda i, w: (0, 0, 0)),
        ]
        + [pl.BlockSpec((GROUP, cells), at_base)] * (2 * chips)
        + [pl.BlockSpec((GROUP, edge), at_base)] * 2
        + [pl.BlockSpec((GROUP, edge), lambda i, w: (last, 0))] * 2
        + [pl.BlockSpec((GROUP, cells), at_base)] * (2 * chips)
        + [pl.BlockSpec((GROUP, edge), lambda i, w: (i, 0))] * 2
    )
    operands = [where, coef, fields, *map(in_hbm, energies), *edges]
    operands += [*map(in_hbm, terms[: 2 * chips]), *terms[2 * chips :]]
    aliases = {}
    kernel = functools.partial(propagate_kernel, chips, halo)
    if previous is not None:
        aliases = {len(operands): 0}
        operands.append(previous)
        in_specs.append(pl.BlockSpec(memory_space=pl.ANY))
    return pl.pallas_call(
        kernel,
        grid_spec=pltpu.PrefetchScalarGridSpec(
            num_scalar_prefetch=1,
            grid=(steps,),
            in_specs=in_specs,
            out_specs=pl.BlockSpec((GROUP * inner, width), lambda i, w: (base + i, 0)),
            scratch_shapes=[
                pltpu.VMEM((rows, width // LANES, GROUP, LANES), jnp.float32),
                pltpu.VMEM((width // LANES, GROUP * inner, LANES), jnp.float32),
                pltpu.VMEM((3, rows, width // LANES, SUBLANES, LANES), jnp.float32),
            ],
        ),
        out_shape=shape,
        input_output_aliases=aliases,
        compiler_params=pltpu.CompilerParams(vmem_limit_bytes=10 * MIB),
        cost_estimate=pl.CostEstimate(
            flops=60 * shape.size * part // local,
            bytes_accessed=8 * shape.size * part // local,
            transcendentals=0,
        ),
        name="propagate",
    )(*operands)


def thirds(value):
    pieces, rest = [], value
    for _ in range(3):
        piece = lax.reduce_precision(rest, 8, 7)
        pieces.append(piece)
        rest = rest - piece
    stacked = jnp.stack(pieces, axis=1).reshape(3 * value.shape[0], value.shape[1])
    return jnp.pad(stacked, ((0, GROUP - stacked.shape[0]), (0, 0))).astype(jnp.bfloat16)


def pair_up(value, start):
    count = lax.axis_size("strip")
    target = list(range(count))
    for i in range(start, count - 1, 2):
        target[i], target[i + 1] = i + 1, i
    return lax.ppermute(value, "strip", list(enumerate(target)))


def per_device_paired(
    energy,
    heading,
    growth,
    courant,
    dissip,
    mixing,
    transfer,
    pattern,
    regime_winds,
    regime,
    seeds,
    sea_mask,
):
    chips = lax.axis_size("comp") // 2
    local, rows, width = energy.shape
    halo = SUBSTEPS
    units = local // GROUP
    parts = (units // 2 * GROUP, (units - units // 2) * GROUP)
    me, strip, strips = lax.axis_index("comp"), lax.axis_index("strip"), lax.axis_size("strip")
    chip, odd = me // 2, strip % 2
    has_above = (strip > 0).astype(jnp.int32)
    has_below = (strip < strips - 1).astype(jnp.int32)
    where = jnp.stack(
        [
            chip,
            me % 2,
            1 - odd,
            odd,
            jnp.where(odd == 1, has_above, has_below),
            jnp.where(odd == 1, has_below, has_above),
        ]
    ).astype(jnp.int32)

    outer = spread(where, energy, chips, halo, True)
    rest = spread(where, energy, chips, halo, False)
    near_outer = [outer[0]] + [exchange(outer[m], "comp", 2 * m) for m in range(1, chips)]
    first, second = weights(where, pattern, mixing, transfer, chips)
    near_outer, rest, first, second = lax.optimization_barrier(
        (near_outer, rest, first, second)
    )
    middle, sides = rest[:chips], rest[chips:]
    near_middle = [middle[0]] + [exchange(middle[m], "comp", 2 * m) for m in range(1, chips)]
    energies = [*outer, *middle] + [pair_up(sides[side], side) for side in range(2)]

    far_outer = [exchange(value, "comp", 1) for value in near_outer]
    sent_outer = source_terms(where, first, second, dissip, near_outer, far_outer)
    landed_outer = [sent_outer[0]] + [
        exchange(sent_outer[m], "comp", 2 * m) for m in range(1, chips)
    ]

    regime_winds, regime, seeds, sea_mask, _ = lax.optimization_barrier(
        (regime_winds, regime, seeds, sea_mask, sent_outer)
    )
    wind_u, wind_v = strip_winds(regime_winds, regime, seeds)
    fields = jnp.stack([wind_u, wind_v, sea_mask.astype(jnp.float32)])
    upper, lower = fields[:, :halo], fields[:, rows - halo :]
    extra = jnp.stack(
        [
            thirds(jnp.where(odd == 1, upper, lower).reshape(3, -1)),
            thirds(jnp.where(odd == 1, lower, upper).reshape(3, -1)),
        ]
    )
    along, across = courant[:, 0], courant[:, 1]
    coef = jnp.stack(
        [
            growth * jnp.cos(heading),
            growth * jnp.sin(heading),
            1.0 - jnp.abs(along) - jnp.abs(across),
            jnp.maximum(along, 0.0),
            -jnp.minimum(along, 0.0),
            jnp.maximum(across, 0.0),
            -jnp.minimum(across, 0.0),
            jnp.zeros_like(along),
        ],
        axis=1,
    )

    near_middle, sent_outer = lax.optimization_barrier((near_middle, sent_outer))
    far_middle = [exchange(value, "comp", 1) for value in near_middle]
    sent_middle = source_terms(where, first, second, dissip, near_middle, far_middle)
    landed_middle = [sent_middle[0]] + [
        exchange(sent_middle[m], "comp", 2 * m) for m in range(1, chips)
    ]

    landed_outer, _ = lax.optimization_barrier((landed_outer, sent_middle))
    edges = gather_edges(where, extra, landed_outer, parts)
    edges = [pair_up(edge, index % 2) for index, edge in enumerate(edges)]
    landed = [*landed_outer, *landed_middle]
    result = None
    for j in range(len(parts)):
        result = propagate(
            where,
            coef,
            fields,
            energies,
            edges[:2],
            landed + edges[2 * j : 2 * j + 2],
            sum(parts[:j]),
            parts[j],
            result,
            halo,
        )
    return result.reshape(local, rows, width)


def solution(mesh):
    placed = (
        P("comp", "strip", None),
        P("comp"),
        P("comp"),
        P("comp", None),
        P(),
        P(),
        P(),
        P(),
        P(),
        P("strip", None),
        P("strip", None),
        P("strip", None),
    )
    paired = mesh.shape["comp"] == 2 * SUBSTEPS
    body = per_device_paired if paired else per_device
    return jax.shard_map(
        body, mesh=mesh, in_specs=placed, out_specs=P("comp", "strip", None), check_vma=False
    )
```
